512 devices in a mesh: wide: 32 (over x, y_hi, core), narrow: 16 (over z, y_lo).
Axes of the slice: x: 4, y: 8 (y_hi: 4, y_lo: 2; y = y_hi * 2 + y_lo), z: 8, core: 2. Of those that a mesh axis runs over, the one named last changes fastest.
Arguments:
- volume: bfloat16 [32, 128, 64, 128], P(None, 'wide', 'narrow'), may hold values from -6 to 6
- cotangent: bfloat16 [32, 128, 64, 128], P(None, 'wide', 'narrow'), may hold values from -6 to 6
- conv_first: bfloat16 [3, 3, 3, 32, 32], replicated, may hold values from -0.21875 to 0.21875
- conv_second: bfloat16 [3, 3, 3, 32, 64], replicated, may hold values from -0.21875 to 0.21875
- conv_bottom: bfloat16 [3, 3, 3, 64, 128], replicated, may hold values from -0.3125 to 0.3125
- lift_weight: bfloat16 [64, 128], replicated, may hold values from -2 to 2
- conv_decode: bfloat16 [3, 3, 3, 64, 32], replicated, may hold values from -0.15625 to 0.15625
- conv_final: bfloat16 [3, 3, 3, 32, 32], replicated, may hold values from -0.21875 to 0.21875
Outputs:
- features_out: bfloat16 [32, 128, 64, 128], P(None, 'wide', 'narrow')
- input_grad: bfloat16 [32, 128, 64, 128], P(None, 'wide', 'narrow')
The draws below stay inside these ranges and needn't reach their ends.
All inputs are finite; a program needn't handle non-finite values.
Results may differ from the reference program's by a relative error of at most 0.013.
Values may be sent and summed in bfloat16 or wider, within the bound.
No kernel may reach another device: no remote copies, remote signals or barrier semaphores. Data moves between devices by JAX's collectives and lax.ppermute only.
A program may use at most 64 MiB of HBM per device.

```python
import jax
import jax.numpy as jnp
from jax import lax

C1 = 32
C2 = 64
C3 = 128
CZ = 128
NX = 128
NY = 64


def block_levels(own_key, dims, cuts, low, largest):
    gain, own = 1.0, jax.random.fold_in(own_key, 6)
    for position, parts in cuts:
        heights = jnp.exp(jax.random.uniform(jax.random.fold_in(own, position), (parts,), jnp.float32, low / len(cuts), largest / len(cuts)))
        gain = gain * jnp.repeat(heights, dims[position] // parts).reshape([-1 if axis == position else 1 for axis in range(len(dims))])
    return gain


def scatter_about(key, shape, width, most, shards=(), kind=jnp.bfloat16):
    entries = jax.random.normal(key, shape, jnp.float32) * width
    if len(shards) > 0:
        entries = block_levels(key, shape, shards, -0.22, 0.18) * entries
    return jnp.clip(entries, min=-most, max=most).astype(kind)


def setup_inputs(seed: int = 0) -> dict:
    keys = jax.random.split(jax.random.key(seed), 9)
    return {
        "volume": scatter_about(keys[0], (C1, NX, NY, CZ), 1.0, 6.0, ((1, 32), (2, 16))),
        "cotangent": scatter_about(keys[1], (C1, NX, NY, CZ), 1.0, 6.0, ((1, 32), (2, 16))),
        "conv_first": scatter_about(keys[2], (3, 3, 3, C1, C1), (27 * C1) ** -0.5, 0.21875),
        "conv_second": scatter_about(keys[3], (3, 3, 3, C1, C2), (27 * C1) ** -0.5, 0.21875),
        "conv_bottom": scatter_about(keys[4], (3, 3, 3, C2, C3), (27 * C2 // 4) ** -0.5, 0.3125),
        "lift_weight": scatter_about(keys[5], (C2, C3), (C3 // 16) ** -0.5, 2.0),
        "conv_decode": scatter_about(keys[6], (3, 3, 3, C2, C1), (27 * C2) ** -0.5, 0.15625),
        "conv_final": scatter_about(keys[7], (3, 3, 3, C1, C1), (27 * C1) ** -0.5, 0.21875),
    }


def conv(field, kernel):
    out = lax.conv_general_dilated(field.astype(jnp.float32)[None], kernel.astype(jnp.float32), (1, 1, 1), "SAME", dimension_numbers=("NCDHW", "DHWIO", "NCDHW"))
    return out[0]


def flipped(kernel):
    return jnp.flip(kernel, (0, 1, 2)).transpose(0, 1, 2, 4, 3)


def blocks(field):
    chans, xs, ys, zs = field.shape
    return field.astype(jnp.float32).reshape(chans, xs // 2, 2, ys // 2, 2, zs // 2, 2)


def pool_mean(field):
    return jnp.mean(blocks(field), axis=(2, 4, 6))


def pool_sum(field):
    return jnp.sum(blocks(field), axis=(2, 4, 6))


def upsample(field):
    return jnp.repeat(jnp.repeat(jnp.repeat(field, 2, 1), 2, 2), 2, 3)


def silu(value):
    return value * jax.nn.sigmoid(value)


def slope(value):
    sig = jax.nn.sigmoid(value)
    return sig * (1.0 + value * (1.0 - sig))


def pointwise(matrix, field):
    chans, xs, ys, zs = field.shape
    flat = field.astype(jnp.float32).reshape(chans, xs * ys * zs)
    out = jnp.dot(matrix.astype(jnp.float32), flat)
    return out.reshape(matrix.shape[0], xs, ys, zs)


def reference(volume, cotangent, conv_first, conv_second, conv_bottom, lift_weight, conv_decode, conv_final):
    bf = jnp.bfloat16
    f32 = jnp.float32
    pre_first = conv(volume, conv_first)
    hidden_first = silu(pre_first).astype(bf)
    pooled_first = pool_mean(hidden_first).astype(bf)
    pre_second = conv(pooled_first, conv_second)
    hidden_second = silu(pre_second).astype(bf)
    pooled_second = pool_mean(hidden_second).astype(bf)
    pre_bottom = conv(pooled_second, conv_bottom)
    hidden_bottom = silu(pre_bottom).astype(bf)
    joined_second = (upsample(pointwise(lift_weight, hidden_bottom)) + hidden_second.astype(f32)).astype(bf)
    pre_decode = conv(joined_second, conv_decode)
    hidden_decode = silu(pre_decode).astype(bf)
    joined_first = (upsample(hidden_decode.astype(f32)) + hidden_first.astype(f32)).astype(bf)
    features_out = conv(joined_first, conv_final).astype(bf)
    grad_joined = conv(cotangent, flipped(conv_final)).astype(bf)
    grad_decode = (pool_sum(grad_joined) * slope(pre_decode)).astype(bf)
    grad_second_up = conv(grad_decode, flipped(conv_decode)).astype(bf)
    grad_lift = pool_sum(grad_second_up).astype(bf)
    grad_bottom = (pointwise(lift_weight.T, grad_lift) * slope(pre_bottom)).astype(bf)
    grad_pool_second = conv(grad_bottom, flipped(conv_bottom))
    grad_second = ((grad_second_up.astype(f32) + upsample(grad_pool_second) / 8.0) * slope(pre_second)).astype(bf)
    grad_pool_first = conv(grad_second, flipped(conv_second))
    grad_first = ((grad_joined.astype(f32) + upsample(grad_pool_first) / 8.0) * slope(pre_first)).astype(bf)
    input_grad = conv(grad_first, flipped(conv_first)).astype(bf)
    return features_out, input_grad
```

```python
import functools

import jax
import jax.numpy as jnp
from jax import lax
from jax.experimental import pallas as pl
from jax.experimental.pallas import tpu as pltpu
from jax.sharding import PartitionSpec as P

bf = jnp.bfloat16
f32 = jnp.float32


def forward_matrix(kernel):
    chans, outs = kernel.shape[3:]
    return kernel.transpose(2, 4, 0, 1, 3).reshape(3 * outs, 9 * chans)


def backward_matrix(kernel):
    chans, outs = kernel.shape[3:]
    return jnp.flip(kernel, (0, 1, 2)).transpose(2, 3, 0, 1, 4).reshape(3 * chans, 9 * outs)


def dot(a, b):
    return jnp.dot(a, b, preferred_element_type=f32)


def lanes(rows, cols=128):
    return lax.broadcasted_iota(jnp.int32, (rows, cols), 1)


def sigma(value):
    return 1.0 / (1.0 + jnp.exp(-value))


def silu(value):
    return value * sigma(value)


def slope(value):
    s = sigma(value)
    return s * (1.0 + value * (1.0 - s))


def zsum(prod, outs, span):
    pos = lanes(outs) & (span - 1)
    first, last = pos == 0, pos == span - 1
    tiles = []
    for start in range(0, prod.shape[1], 128):
        cut = slice(start, start + 128)
        below = pltpu.roll(prod[:outs, cut], 1, 1)
        above = pltpu.roll(prod[2 * outs :, cut], 127, 1)
        tiles.append(
            prod[outs : 2 * outs, cut]
            + jnp.where(first, 0.0, below)
            + jnp.where(last, 0.0, above)
        )
    return tiles


def rows_of(tiles):
    return jnp.concatenate(tiles, axis=0)


def cols_of(tiles):
    return jnp.concatenate(tiles, axis=1)


def flag(block, count):
    return jnp.where((block >= 0) & (block < count), 1.0, 0.0).astype(f32)


def selection(rows, cols, target):
    r = lax.broadcasted_iota(jnp.int32, (rows, cols), 0)
    c = lax.broadcasted_iota(jnp.int32, (rows, cols), 1)
    return jnp.where(target(r, c), 1.0, 0.0).astype(bf)


def pair_pool():
    return selection(1024, 128, lambda r, c: (r >> 9) * 64 + ((r & 127) >> 1) == c)


def pair_up():
    return selection(
        128, 256, lambda r, c: (r >> 6 == c >> 7) & ((r & 63) == (c & 127) >> 1)
    )


def block_up():
    return selection(
        128, 512, lambda r, c: (r >> 5 == c >> 7) & ((r & 31) == (c & 63) >> 1)
    )


def split(value):
    high = value.astype(bf)
    low = (value - high.astype(f32)).astype(bf)
    return rows_of([high, low])


def exact_up(value, matrix):
    rows = value.shape[0]
    out = dot(split(value), matrix)
    return out[:rows] + out[rows:]


def cross(left, right):
    low = lanes(left.shape[0]) < 64
    out = jnp.where(
        low, pltpu.roll(left.astype(f32), 64, 1), pltpu.roll(right.astype(f32), 64, 1)
    )
    return out.astype(left.dtype)


def neighbours(tiles, keep):
    chans = tiles[0].shape[0]
    seg = lanes(chans) >> 5
    masked = [t.astype(f32) * k for t, k in zip(tiles, keep)]
    cache = {}

    def rolled(q, amount):
        if (q, amount) not in cache:
            cache[q, amount] = (
                masked[q] if amount == 0 else pltpu.roll(masked[q], amount, 1)
            )
        return cache[q, amount]

    taps = []
    for dx in range(3):
        for dy in range(3):
            out = None
            for t in range(4):
                x, y = t // 2 + dx, t % 2 + dy
                q, s = (x // 2) * 2 + y // 2, (x % 2) * 2 + y % 2
                piece = rolled(q, (t - s) * 32 % 128)
                out = piece if out is None else jnp.where(seg == t, piece, out)
            taps.append(out.astype(bf))
    return rows_of(taps)


def quadrant_keep(chans, base_x, base_y, count_x, count_y):
    pos = lanes(chans)
    a, b = pos >> 6, (pos >> 5) & 1
    keep = []
    for q in range(4):
        x, y = base_x + 2 * (q // 2) + a, base_y + 2 * (q % 2) + b
        inside = (x >= 0) & (x < count_x) & (y >= 0) & (y < count_y)
        keep.append(jnp.where(inside, 1.0, 0.0).astype(f32))
    return keep


def place(pos_ref):
    return pos_ref[0], pos_ref[1]


def columns(field, x, y):
    return rows_of([field[x + dx, y + dy] for dx in range(3) for dy in range(3)])


def encode(
    counts, pos, vol, vol_l, vol_r, cot, cot_l, cot_r, first, second, final_b,
    hid, pre, gj, content2, p2, ev, ec, h8,
):
    w, n = place(pos)
    ev[0:3], ev[3:7], ev[7:10] = vol_l[...], vol[...], vol_r[...]
    ec[0:2], ec[2:6], ec[6:8] = cot_l[...], cot[...], cot_r[...]

    def row(x, keep):
        prod = dot(first[...], cols_of([columns(ev, x, y) for y in range(8)]))
        for y, value in enumerate(zsum(prod, 32, 128)):
            h = silu(value).astype(bf)
            h8[x, y] = h
            if keep and 1 <= y <= 6:
                hid[x - 1, y - 1] = h
                pre[x - 1, y - 1] = value

    row(0, False)
    pl.loop(1, 7)(lambda x: row(x, True))
    row(7, False)

    @pl.loop(0, 6)
    def _(x):
        prod = dot(final_b[...], cols_of([columns(ec, x, y) for y in range(6)]))
        for y, value in enumerate(zsum(prod, 32, 128)):
            gj[x, y] = value.astype(bf)

    pool = pair_pool()
    pick = lambda field, x, y: cols_of(
        [field[x + i, y + j] for j in range(2) for i in range(2)]
    )
    sums = rows_of(
        [cols_of([pick(gj, 1 + 2 * x, 1), pick(gj, 1 + 2 * x, 3)]) for x in range(2)]
    )
    content2[128:192] = dot(sums, pool).astype(bf)

    parts = rows_of(
        [
            cols_of([pick(h8, 2 * x, 2 * y), pick(h8, 2 * x, 2 * y + 2)])
            for x in range(4)
            for y in range(3)
        ]
    )
    pooled = dot(parts, pool) * 0.125
    low = lanes(32) < 64
    fx = [flag(w - 1, counts[0]), 1.0, 1.0, flag(w + 1, counts[0])]
    fl, fr = flag(n - 1, counts[1]), flag(n + 1, counts[1])
    fy = [jnp.where(low, fl, 1.0), jnp.ones((32, 128), f32), jnp.where(low, 1.0, fr)]
    tile = [
        [
            (pooled[(x * 3 + y) * 32 : (x * 3 + y + 1) * 32] * fy[y] * fx[x]).astype(bf)
            for y in range(3)
        ]
        for x in range(4)
    ]
    stack = [rows_of([tile[x + dx][y] for dx in range(3) for y in range(3)]) for x in range(2)]
    pre2 = zsum(dot(second[...], cols_of(stack)), 64, 64)
    spread = selection(256, 128, lambda r, c: (r & 63) >> 1 == (c & 31))
    hidden2 = cols_of([silu(v).astype(bf) for v in pre2])
    p2[...] = (dot(hidden2, spread) * 0.125).astype(bf)
    for x in range(2):
        content2[64 * x : 64 * x + 64] = pre2[x].astype(bf)


def bottom(counts, pos, got, weight, lift, out):
    w, n = place(pos)
    bx, by = 2 * ((w + 1) // 2) - 2, 2 * ((n + 1) // 2) - 2
    keep = quadrant_keep(64, bx, by, *counts)
    taps = neighbours([got[q, 192:256] for q in range(4)], keep)
    (pre,) = zsum(dot(weight[...], taps), 128, 32)
    lifted = dot(lift[...], silu(pre).astype(bf))
    up = exact_up(lifted, block_up())
    grad = slope(pre)
    odd = (lanes(128) >> 5) & 1 == 1
    turned = jnp.where(odd, pltpu.roll(grad, 96, 1), pltpu.roll(grad, 32, 1)).astype(bf)
    for t in range(4):
        out[t, 512:640] = turned
    for s in range(4):
        for x in range(2):
            hidden = silu(got[s, 64 * x : 64 * x + 64].astype(f32)).astype(bf)
            joined = (up[:, 128 * s : 128 * s + 128] + hidden.astype(f32)).astype(bf)
            at = (2 * s + x) * 64
            for t in range(4):
                out[t, at : at + 64] = joined
        sums = got[s, 128:192]
        for t in range(4):
            out[t, 640 + 64 * s : 704 + 64 * s] = sums


def spread_quadrants(got, start, rows, base_x, base_y, counts, store):
    for row in range(8):
        for pair in range(4):
            q, s = (row // 4) * 2 + pair // 2, ((row % 4) // 2) * 2 + pair % 2
            at = start + (2 * s + row % 2) * rows
            tile = got[q, at : at + rows]
            edge = None
            if row // 2 in (0, 3):
                edge = flag(base_x + row // 2, counts[0])
            if pair in (0, 3):
                other = flag(base_y + pair, counts[1])
                edge = other if edge is None else edge * other
            if edge is not None:
                tile = (tile.astype(f32) * edge).astype(bf)
            store(row, pair, tile)


def decode(
    counts, pos, got, hid, weight, weight_b, lift_t, final,
    feat, out, dom, mid, sums, pd, gd, gs, jf,
):
    w, n = place(pos)
    ra, rb = w & 1, n & 1
    bx, by = w - ra - 1, n - rb - 1

    def put(row, pair, tile):
        dom[row, pair] = tile

    def put_sum(row, pair, tile):
        sums[row, pair] = tile

    spread_quadrants(got, 0, 64, bx, by, counts, put)
    spread_quadrants(got, 640, 32, bx, by, counts, put_sum)

    @pl.loop(0, 8)
    def _(row):
        for o in range(3):
            mid[row, o] = cross(dom[row, o], dom[row, o + 1])

    @pl.loop(0, 6)
    def _(i):
        stack = []
        for o in range(3):
            taps = []
            for dx in range(3):
                taps += [dom[i + dx, o], mid[i + dx, o], dom[i + dx, o + 1]]
            stack.append(rows_of(taps))
        for o, value in enumerate(zsum(dot(weight[...], cols_of(stack)), 32, 64)):
            pd[i, o] = value
            total = cross(sums[i + 1, o].astype(f32), sums[i + 1, o + 1].astype(f32))
            gd[i, o] = (total * slope(value)).astype(bf)

    @pl.loop(0, 4)
    def _(j):
        stack = []
        for p in range(2):
            taps = []
            for dx in range(3):
                left, right = gd[j + dx, p], gd[j + dx, p + 1]
                taps += [left, cross(left, right), right]
            stack.append(rows_of(taps))
        for p, value in enumerate(zsum(dot(weight_b[...], cols_of(stack)), 64, 64)):
            gs[j, p] = value.astype(bf)

    parts = cols_of(
        [gs[2 * a + x, b] for a in range(2) for b in range(2) for x in range(2)]
    )
    gather = selection(1024, 128, lambda r, c: (r >> 8) * 32 + ((r & 63) >> 1) == c)
    grad_lift = dot(parts, gather).astype(bf)
    seg = lanes(128) >> 5
    grad = got[0, 512:640].astype(f32)
    for q in range(1, 4):
        grad = jnp.where(seg == q, got[q, 512:640].astype(f32), grad)
    grad_bottom = (dot(lift_t[...], grad_lift) * grad).astype(bf)
    for t in range(4):
        out[t, 0:128] = grad_bottom
        for x in range(2):
            out[t, 128 + 64 * x : 192 + 64 * x] = gs[2 * ra + x, rb]

    hidden = rows_of(
        [silu(pd[2 * ra + r, rb + o]).astype(bf) for r in range(4) for o in range(2)]
    )
    up = dot(hidden, pair_up())
    fx = [flag(w - 1, counts[0]), None, None, None, None, flag(w + 1, counts[0])]
    fy = [flag(n - 1, counts[1]), None, None, None, None, flag(n + 1, counts[1])]
    for x in range(6):
        for y in range(6):
            r, m = (x + 1) // 2, (y + 1) // 2
            at = (2 * r + m // 2) * 32
            value = up[at : at + 32, 128 * (m % 2) : 128 * (m % 2) + 128]
            value = value + hid[x, y].astype(f32)
            for edge in (fx[x], fy[y]):
                value = value if edge is None else value * edge
            jf[x, y] = value.astype(bf)

    @pl.loop(0, 4)
    def _(x):
        prod = dot(final[...], cols_of([columns(jf, x, y) for y in range(4)]))
        for y, value in enumerate(zsum(prod, 32, 128)):
            feat[x, y] = value.astype(bf)


def deep_gradient(counts, pos, got, early, weight, out):
    w, n = place(pos)
    bx, by = 2 * ((w + 1) // 2) - 2, 2 * ((n + 1) // 2) - 2
    keep = quadrant_keep(128, bx, by, *counts)
    taps = neighbours([got[q, 0:128] for q in range(4)], keep)
    (pooled,) = zsum(dot(weight[...], taps), 64, 32)
    up = exact_up(pooled * 0.125, block_up())
    for s in range(4):
        for x in range(2):
            grad = slope(early[s, 64 * x : 64 * x + 64].astype(f32))
            above = got[s, 128 + 64 * x : 192 + 64 * x].astype(f32)
            value = ((above + up[:, 128 * s : 128 * s + 128]) * grad).astype(bf)
            at = (2 * s + x) * 64
            for t in range(4):
                out[t, at : at + 64] = value


def finish(counts, pos, got, gj, pre, second_b, first_b, out, dom, gf):
    w, n = place(pos)
    ra, rb = w & 1, n & 1

    def put(row, pair, tile):
        dom[row, pair] = tile

    spread_quadrants(got, 0, 64, w - ra - 1, n - rb - 1, counts, put)
    own = [[dom[2 * ra + row, rb + p] for p in range(3)] for row in range(6)]
    mixed = [[cross(line[o], line[o + 1]) for o in range(2)] for line in own]
    grads = []
    for r in range(4):
        stack = []
        for o in range(2):
            taps = []
            for dx in range(3):
                taps += [own[r + dx][o], mixed[r + dx][o], own[r + dx][o + 1]]
            stack.append(rows_of(taps))
        grads += zsum(dot(second_b[...], cols_of(stack)), 32, 64)
    up = exact_up(rows_of(grads) * 0.125, pair_up())
    fx = [flag(w - 1, counts[0]), None, None, None, None, flag(w + 1, counts[0])]
    fy = [flag(n - 1, counts[1]), None, None, None, None, flag(n + 1, counts[1])]
    for x in range(6):
        for y in range(6):
            r, m = (x + 1) // 2, (y + 1) // 2
            at = (2 * r + m // 2) * 32
            value = up[at : at + 32, 128 * (m % 2) : 128 * (m % 2) + 128]
            value = (value + gj[x, y].astype(f32)) * slope(pre[x, y])
            for edge in (fx[x], fy[y]):
                value = value if edge is None else value * edge
            gf[x, y] = value.astype(bf)

    @pl.loop(0, 4)
    def _(x):
        prod = dot(first_b[...], cols_of([columns(gf, x, y) for y in range(4)]))
        for y, value in enumerate(zsum(prod, 32, 128)):
            out[x, y] = value.astype(bf)


def call(body, counts, outs, scratch, *args):
    smem = pl.BlockSpec(memory_space=pltpu.SMEM)
    vmem = pl.BlockSpec(memory_space=pltpu.VMEM)
    return pl.pallas_call(
        functools.partial(body, counts),
        out_shape=[jax.ShapeDtypeStruct(s, d) for s, d in outs],
        in_specs=[smem] + [vmem] * (len(args) - 1),
        out_specs=[vmem] * len(outs),
        scratch_shapes=[pltpu.VMEM(s, d) for s, d in scratch],
        compiler_params=pltpu.CompilerParams(vmem_limit_bytes=48 * 1024 * 1024),
        name=body.__name__,
    )(*args)


def send(cells, axis, step):
    count = lax.axis_size(axis)
    pairs = [(i, i + step) for i in range(count) if 0 <= i + step < count]
    return lax.ppermute(cells, axis, pairs)


def widened(cells, axis, dim, width):
    size = cells.shape[dim]
    head = lax.slice_in_dim(cells, 0, width, axis=dim)
    tail = lax.slice_in_dim(cells, size - width, size, axis=dim)
    return send(tail, axis, 1), send(head, axis, -1)


def shards(
    volume, cotangent, conv_first, conv_second, conv_bottom, lift_weight, conv_decode, conv_final
):
    counts = (lax.axis_size("wide"), lax.axis_size("narrow"))
    pos = jnp.stack([lax.axis_index("wide"), lax.axis_index("narrow")]).astype(jnp.int32)

    def gathered(content, shift):
        groups = [
            [
                ((i + a) % counts[0]) * counts[1] + (j + b) % counts[1]
                for a in range(2)
                for b in range(2)
            ]
            for i in range(shift, counts[0] + shift, 2)
            for j in range(shift, counts[1] + shift, 2)
        ]
        return lax.all_to_all(
            content, ("wide", "narrow"), 0, 0, axis_index_groups=groups
        )

    vol = volume.transpose(1, 2, 0, 3)
    cot = cotangent.transpose(1, 2, 0, 3)
    vl, vr = widened(vol, "narrow", 1, 3)
    cl, cr = widened(cot, "narrow", 1, 2)
    vol = jnp.concatenate([vl, vol, vr], axis=1)
    cot = jnp.concatenate([cl, cot, cr], axis=1)
    vol_l, vol_r = widened(vol, "wide", 0, 3)
    cot_l, cot_r = widened(cot, "wide", 0, 2)

    full = (6, 6, 32, 128)
    hid, pre, gj, content, p2 = call(
        encode, counts,
        [(full, bf), (full, f32), (full, bf), ((192, 128), bf), ((64, 128), bf)],
        [((10, 10, 32, 128), bf), ((8, 8, 32, 128), bf), ((8, 8, 32, 128), bf)],
        pos, vol, vol_l, vol_r, cot, cot_l, cot_r,
        forward_matrix(conv_first), forward_matrix(conv_second), backward_matrix(conv_final),
    )
    four = gathered(jnp.broadcast_to(p2, (4, 64, 128)), 0)
    seg = lax.broadcasted_iota(jnp.int32, (64, 128), 1) // 32
    packed = four[0]
    for q in range(1, 4):
        packed = jnp.where(seg == q, four[q], packed)
    content = jnp.concatenate([content, packed], axis=0)
    early = gathered(jnp.broadcast_to(content, (4, 256, 128)), 1)
    (content,) = call(
        bottom, counts, [((4, 896, 128), bf)], [],
        pos, early, forward_matrix(conv_bottom), lift_weight,
    )
    got = gathered(content, 0)
    cells = (4, 4, 32, 128)
    features, content = call(
        decode, counts, [(cells, bf), ((4, 256, 128), bf)],
        [
            ((8, 4, 64, 128), bf), ((8, 3, 64, 128), bf), ((8, 4, 32, 128), bf),
            ((6, 3, 32, 128), f32), ((6, 3, 32, 128), bf), ((4, 2, 64, 128), bf),
            (full, bf),
        ],
        pos, got, hid, forward_matrix(conv_decode), backward_matrix(conv_decode),
        lift_weight.T, forward_matrix(conv_final),
    )
    got = gathered(content, 1)
    (content,) = call(
        deep_gradient, counts, [((4, 512, 128), bf)], [],
        pos, got, early, backward_matrix(conv_bottom),
    )
    got = gathered(content, 0)
    (grad,) = call(
        finish, counts, [(cells, bf)], [((8, 4, 64, 128), bf), (full, bf)],
        pos, got, gj, pre, backward_matrix(conv_second), backward_matrix(conv_first),
    )
    return features.transpose(2, 0, 1, 3), grad.transpose(2, 0, 1, 3)


def solution(mesh):
    field = P(None, "wide", "narrow", None)
    return jax.shard_map(
        shards,
        mesh=mesh,
        in_specs=(field, field) + (P(),) * 6,
        out_specs=(field, field),
        check_vma=False,
    )
```

```python
import functools

import jax
import jax.numpy as jnp
from jax import lax
from jax.experimental import pallas as pl
from jax.experimental.pallas import tpu as pltpu
from jax.sharding import PartitionSpec as P

bf = jnp.bfloat16
f32 = jnp.float32


def forward_matrix(kernel):
    chans, outs = kernel.shape[3:]
    return kernel.transpose(2, 4, 0, 1, 3).reshape(3 * outs, 9 * chans)


def backward_matrix(kernel):
    chans, outs = kernel.shape[3:]
    return jnp.flip(kernel, (0, 1, 2)).transpose(2, 3, 0, 1, 4).reshape(3 * chans, 9 * outs)


def forward_strips(kernel):
    chans, outs = kernel.shape[3:]
    return kernel.transpose(0, 2, 4, 1, 3).reshape(3, 3 * outs, 3 * chans)


def backward_strips(kernel):
    chans, outs = kernel.shape[3:]
    return jnp.flip(kernel, (0, 1, 2)).transpose(0, 2, 3, 1, 4).reshape(3, 3 * chans, 3 * outs)


def dot(a, b):
    return jnp.dot(a, b, preferred_element_type=f32)


def lanes(rows, cols=128):
    return lax.broadcasted_iota(jnp.int32, (rows, cols), 1)


def sigma(value):
    return 1.0 / (1.0 + jnp.exp(-value))


def silu(value):
    return value * sigma(value)


def slope(value):
    s = sigma(value)
    return s * (1.0 + value * (1.0 - s))


def zsum(prod, outs, span):
    pos = lanes(outs) & (span - 1)
    first, last = pos == 0, pos == span - 1
    tiles = []
    for start in range(0, prod.shape[1], 128):
        cut = slice(start, start + 128)
        below = pltpu.roll(prod[:outs, cut], 1, 1)
        above = pltpu.roll(prod[2 * outs :, cut], 127, 1)
        tiles.append(
            prod[outs : 2 * outs, cut]
            + jnp.where(first, 0.0, below)
            + jnp.where(last, 0.0, above)
        )
    return tiles


def rows_of(tiles):
    return jnp.concatenate(tiles, axis=0)


def cols_of(tiles):
    return jnp.concatenate(tiles, axis=1)


def flag(block, count):
    return jnp.where((block >= 0) & (block < count), 1.0, 0.0).astype(f32)


def selection(rows, cols, target):
    r = lax.broadcasted_iota(jnp.int32, (rows, cols), 0)
    c = lax.broadcasted_iota(jnp.int32, (rows, cols), 1)
    return jnp.where(target(r, c), 1.0, 0.0).astype(bf)


def pair_pool():
    return selection(1024, 128, lambda r, c: (r >> 9) * 64 + ((r & 127) >> 1) == c)


def pair_up():
    return selection(
        128, 256, lambda r, c: (r >> 6 == c >> 7) & ((r & 63) == (c & 127) >> 1)
    )


def block_up():
    return selection(
        128, 512, lambda r, c: (r >> 5 == c >> 7) & ((r & 31) == (c & 63) >> 1)
    )


def split(value):
    high = value.astype(bf)
    low = (value - high.astype(f32)).astype(bf)
    return rows_of([high, low])


def exact_up(value, matrix):
    rows = value.shape[0]
    out = dot(split(value), matrix)
    return out[:rows] + out[rows:]


def cross(left, right):
    low = lanes(left.shape[0]) < 64
    out = jnp.where(
        low, pltpu.roll(left.astype(f32), 64, 1), pltpu.roll(right.astype(f32), 64, 1)
    )
    return out.astype(left.dtype)


def neighbours(tiles, keep):
    chans = tiles[0].shape[0]
    seg = lanes(chans) >> 5
    masked = [t.astype(f32) * k for t, k in zip(tiles, keep)]
    cache = {}

    def rolled(q, amount):
        if (q, amount) not in cache:
            cache[q, amount] = (
                masked[q] if amount == 0 else pltpu.roll(masked[q], amount, 1)
            )
        return cache[q, amount]

    taps = []
    for dx in range(3):
        for dy in range(3):
            out = None
            for t in range(4):
                x, y = t // 2 + dx, t % 2 + dy
                q, s = (x // 2) * 2 + y // 2, (x % 2) * 2 + y % 2
                piece = rolled(q, (t - s) * 32 % 128)
                out = piece if out is None else jnp.where(seg == t, piece, out)
            taps.append(out.astype(bf))
    return rows_of(taps)


def quadrant_keep(chans, base_x, base_y, count_x, count_y):
    pos = lanes(chans)
    a, b = pos >> 6, (pos >> 5) & 1
    keep = []
    for q in range(4):
        x, y = base_x + 2 * (q // 2) + a, base_y + 2 * (q % 2) + b
        inside = (x >= 0) & (x < count_x) & (y >= 0) & (y < count_y)
        keep.append(jnp.where(inside, 1.0, 0.0).astype(f32))
    return keep


def place(pos_ref):
    return pos_ref[0], pos_ref[1]


def square_matrix(strips, out):
    blank = jnp.zeros((96, 128), bf)
    tail = jnp.zeros((96, 32), bf)
    plain = [cols_of([strips[dx], tail]) for dx in range(3)]
    moved = [pltpu.roll(t.astype(f32), 32, 1).astype(bf) for t in plain]
    for i in range(2):
        for j in range(2):
            for u in range(4):
                tile = (moved if j else plain)[u - i] if 0 <= u - i < 3 else blank
                at = 96 * (2 * i + j)
                out[at : at + 96, 128 * u : 128 * u + 128] = tile


def squares(weight, field, x, count):
    taps = [
        rows_of([field[x + u, y + v] for u in range(4) for v in range(4)])
        for y in range(0, count, 2)
    ]
    prod = dot(weight[...], cols_of(taps))
    for k in range(4):
        tiles = zsum(prod[96 * k : 96 * k + 96], 32, 128)
        for at, tile in enumerate(tiles):
            yield k // 2, 2 * at + k % 2, tile


def picked(field, x, y):
    return cols_of([field[x + i, y + j] for j in range(2) for i in range(2)])


def adjoint(counts, pos, cot, cot_l, cot_r, strips, gj, total, ec, matrix):
    square_matrix(strips, matrix)
    ec[0:2], ec[2:6], ec[6:8] = cot_l[...], cot[...], cot_r[...]

    @pl.loop(0, 3)
    def _(i):
        for dx, y, value in squares(matrix, ec, 2 * i, 6):
            gj[2 * i + dx, y] = value.astype(bf)

    sums = rows_of(
        [
            cols_of([picked(gj, 1 + 2 * x, 1), picked(gj, 1 + 2 * x, 3)])
            for x in range(2)
        ]
    )
    total[...] = dot(sums, pair_pool()).astype(bf)


def encode(
    counts, pos, vol, vol_l, vol_r, strips, second,
    hid, pre, early, p2, ev, h8, pre8, matrix,
):
    square_matrix(strips, matrix)
    w, n = place(pos)
    ev[0:3], ev[3:7], ev[7:10] = vol_l[...], vol[...], vol_r[...]

    @pl.loop(0, 4)
    def _(i):
        for dx, y, value in squares(matrix, ev, 2 * i, 8):
            h8[2 * i + dx, y] = silu(value).astype(bf)
            if 1 <= y <= 6:
                pre8[2 * i + dx, y - 1] = value

    hid[...] = h8[1:7, 1:7]
    pre[...] = pre8[1:7]
    parts = rows_of(
        [
            cols_of([picked(h8, 2 * x, 2 * y), picked(h8, 2 * x, 2 * y + 2)])
            for x in range(4)
            for y in range(3)
        ]
    )
    pooled = dot(parts, pair_pool()) * 0.125
    low = lanes(32) < 64
    fx = [flag(w - 1, counts[0]), 1.0, 1.0, flag(w + 1, counts[0])]
    fl, fr = flag(n - 1, counts[1]), flag(n + 1, counts[1])
    fy = [jnp.where(low, fl, 1.0), jnp.ones((32, 128), f32), jnp.where(low, 1.0, fr)]
    tile = [
        [
            (pooled[(x * 3 + y) * 32 : (x * 3 + y + 1) * 32] * fy[y] * fx[x]).astype(bf)
            for y in range(3)
        ]
        for x in range(4)
    ]
    stack = [rows_of([tile[x + dx][y] for dx in range(3) for y in range(3)]) for x in range(2)]
    pre2 = zsum(dot(second[...], cols_of(stack)), 64, 64)
    spread = selection(256, 128, lambda r, c: (r & 63) >> 1 == (c & 31))
    hidden2 = cols_of([silu(v).astype(bf) for v in pre2])
    pooled2 = (dot(hidden2, spread) * 0.125).astype(bf)
    for t in range(4):
        p2[t] = pooled2
    for x in range(2):
        early[64 * x : 64 * x + 64] = pre2[x].astype(bf)


def bottom(counts, pos, got, weight, lift, out):
    w, n = place(pos)
    bx, by = 2 * ((w + 1) // 2) - 2, 2 * ((n + 1) // 2) - 2
    keep = quadrant_keep(64, bx, by, *counts)
    taps = neighbours([got[q, 192:256] for q in range(4)], keep)
    (pre,) = zsum(dot(weight[...], taps), 128, 32)
    lifted = dot(lift[...], silu(pre).astype(bf))
    up = exact_up(lifted, block_up())
    grad = slope(pre)
    ra, rb = w & 1, n & 1
    own = (1 - ra) * 2 + 1 - rb
    seg = lanes(32) >> 5
    packed = None
    for k in range(4):
        moved = pltpu.roll(grad[32 * k : 32 * k + 32], ((k - own) * 32) & 127, 1)
        packed = moved if packed is None else jnp.where(seg == k, moved, packed)
    for t in range(4):
        out[t, 512:544] = packed.astype(bf)
    for s in range(4):
        for x in range(2):
            hidden = silu(got[s, 64 * x : 64 * x + 64].astype(f32)).astype(bf)
            joined = (up[:, 128 * s : 128 * s + 128] + hidden.astype(f32)).astype(bf)
            at = (2 * s + x) * 64
            for t in range(4):
                out[t, at : at + 64] = joined
    for r in range(3):
        row = 1 - ra + r
        for b in range(2):
            start = pl.multiple_of(128 + 32 * (row & 1), 32)
            sums = got[(row >> 1) * 2 + b, pl.ds(start, 32)]
            for t in range(4):
                out[t, 544 + 64 * r + 32 * b : 576 + 64 * r + 32 * b] = sums


def spread_quadrants(got, place_of, rows, base_x, base_y, counts, store):
    for row in range(8):
        for pair in range(4):
            q, at = (row // 4) * 2 + pair // 2, place_of(row, pair)
            if at is None:
                continue
            tile = got[q, at : at + rows]
            edge = None
            if row // 2 in (0, 3):
                edge = flag(base_x + row // 2, counts[0])
            if pair in (0, 3):
                other = flag(base_y + pair, counts[1])
                edge = other if edge is None else edge * other
            if edge is not None:
                tile = (tile.astype(f32) * edge).astype(bf)
            store(row, pair, tile)


def decode(
    counts, pos, got, weight, weight_b, lift_t, out, hidden, dom, mid, sums, pd, gd, gs
):
    w, n = place(pos)
    ra, rb = w & 1, n & 1
    bx, by = w - ra - 1, n - rb - 1

    def put(row, pair, tile):
        dom[row, pair] = tile

    def put_sum(row, pair, tile):
        sums[row - 1, pair] = tile

    def joined_at(row, pair):
        return (((row % 4) // 2 * 2 + pair % 2) * 2 + row % 2) * 64

    def sum_at(row, pair):
        if row in (0, 7):
            return None
        return 544 + ((row - 1) % 3) * 64 + pair % 2 * 32

    spread_quadrants(got, joined_at, 64, bx, by, counts, put)
    spread_quadrants(got, sum_at, 32, bx, by, counts, put_sum)

    @pl.loop(0, 8)
    def _(row):
        for o in range(3):
            mid[row, o] = cross(dom[row, o], dom[row, o + 1])

    @pl.loop(0, 6)
    def _(i):
        stack = []
        for o in range(3):
            taps = []
            for dx in range(3):
                taps += [dom[i + dx, o], mid[i + dx, o], dom[i + dx, o + 1]]
            stack.append(rows_of(taps))
        for o, value in enumerate(zsum(dot(weight[...], cols_of(stack)), 32, 64)):
            pd[i, o] = value
            total = cross(sums[i, o].astype(f32), sums[i, o + 1].astype(f32))
            gd[i, o] = (total * slope(value)).astype(bf)

    @pl.loop(0, 4)
    def _(j):
        stack = []
        for p in range(2):
            taps = []
            for dx in range(3):
                left, right = gd[j + dx, p], gd[j + dx, p + 1]
                taps += [left, cross(left, right), right]
            stack.append(rows_of(taps))
        for p, value in enumerate(zsum(dot(weight_b[...], cols_of(stack)), 64, 64)):
            gs[j, p] = value.astype(bf)

    parts = cols_of(
        [gs[2 * a + x, b] for a in range(2) for b in range(2) for x in range(2)]
    )
    gather = selection(1024, 128, lambda r, c: (r >> 8) * 32 + ((r & 63) >> 1) == c)
    grad_lift = dot(parts, gather).astype(bf)
    seg = lanes(32) >> 5
    packs = [got[q, 512:544].astype(f32) for q in range(4)]
    grads = []
    for k in range(4):
        grad = None
        for q in range(4):
            piece = pltpu.roll(packs[q], (q - k) * 32 % 128, 1) if q != k else packs[q]
            grad = piece if grad is None else jnp.where(seg == q, piece, grad)
        grads.append(grad)
    grad_bottom = (dot(lift_t[...], grad_lift) * rows_of(grads)).astype(bf)
    for t in range(4):
        out[t, 0:128] = grad_bottom
        for x in range(2):
            out[t, 128 + 64 * x : 192 + 64 * x] = gs[2 * ra + x, rb]
    for r in range(4):
        for o in range(2):
            at = (2 * r + o) * 32
            hidden[at : at + 32] = silu(pd[2 * ra + r, rb + o]).astype(bf)


def edges(pos, counts):
    w, n = place(pos)
    fx = [flag(w - 1, counts[0]), None, None, None, None, flag(w + 1, counts[0])]
    fy = [flag(n - 1, counts[1]), None, None, None, None, flag(n + 1, counts[1])]
    return fx, fy


def output(counts, pos, hidden, hid, strips, feat, jf, matrix):
    square_matrix(strips, matrix)
    up = dot(hidden[...], pair_up())
    fx, fy = edges(pos, counts)
    for x in range(6):
        for y in range(6):
            r, m = (x + 1) // 2, (y + 1) // 2
            at = (2 * r + m // 2) * 32
            value = up[at : at + 32, 128 * (m % 2) : 128 * (m % 2) + 128]
            value = value + hid[x, y].astype(f32)
            for edge in (fx[x], fy[y]):
                value = value if edge is None else value * edge
            jf[x, y] = value.astype(bf)

    @pl.loop(0, 2)
    def _(i):
        for dx, y, value in squares(matrix, jf, 2 * i, 4):
            feat[2 * i + dx, y] = value.astype(bf)


def deep_gradient(counts, pos, got, early, weight, out, mine):
    w, n = place(pos)
    bx, by = 2 * ((w + 1) // 2) - 2, 2 * ((n + 1) // 2) - 2
    keep = quadrant_keep(128, bx, by, *counts)
    taps = neighbours([got[q, 0:128] for q in range(4)], keep)
    (pooled,) = zsum(dot(weight[...], taps), 64, 32)
    up = exact_up(pooled * 0.125, block_up())
    for s in range(4):
        for x in range(2):
            grad = slope(early[s, 64 * x : 64 * x + 64].astype(f32))
            above = got[s, 128 + 64 * x : 192 + 64 * x].astype(f32)
            value = ((above + up[:, 128 * s : 128 * s + 128]) * grad).astype(bf)
            mine[2 * s + x] = value
    ra, rb = w & 1, n & 1
    for t in range(4):
        for k in range(2):
            a = jnp.where(ra == t // 2, k, 1 - ra)
            b = jnp.where(rb == t % 2, k, 1 - rb)
            for x in range(2):
                at = (2 * k + x) * 64
                out[t, at : at + 64] = mine[(2 * a + b) * 2 + x]


def finish(counts, pos, got, mine, gj, pre, second_b, strips, out, dom, gf, matrix):
    square_matrix(strips, matrix)
    w, n = place(pos)
    ra, rb = w & 1, n & 1

    def put(x, y, tiles):
        inside = flag(w + x - 1, counts[0]) * flag(n + y - 1, counts[1])
        for i, tile in enumerate(tiles):
            dom[2 * x + i, y] = (tile.astype(f32) * inside).astype(bf)

    far_x, far_y = 2 * (1 - ra), 2 * (1 - rb)
    part = lambda q, k: [got[q, (2 * k + i) * 64 : (2 * k + i) * 64 + 64] for i in range(2)]
    for a in range(2):
        for b in range(2):
            put(a + ra, b + rb, [mine[(2 * a + b) * 2 + i] for i in range(2)])
    for k in range(2):
        put(far_x, k + rb, part(2 * (1 - ra) + rb, k))
        put(k + ra, far_y, part(2 * ra + 1 - rb, k))
    put(far_x, far_y, part(2 * (1 - ra) + 1 - rb, 0))
    own = [[dom[row, p] for p in range(3)] for row in range(6)]
    mixed = [[cross(line[o], line[o + 1]) for o in range(2)] for line in own]
    grads = []
    for r in range(4):
        stack = []
        for o in range(2):
            taps = []
            for dx in range(3):
                taps += [own[r + dx][o], mixed[r + dx][o], own[r + dx][o + 1]]
            stack.append(rows_of(taps))
        grads += zsum(dot(second_b[...], cols_of(stack)), 32, 64)
    up = exact_up(rows_of(grads) * 0.125, pair_up())
    fx, fy = edges(pos, counts)
    for x in range(6):
        for y in range(6):
            r, m = (x + 1) // 2, (y + 1) // 2
            at = (2 * r + m // 2) * 32
            value = up[at : at + 32, 128 * (m % 2) : 128 * (m % 2) + 128]
            value = (value + gj[x, y].astype(f32)) * slope(pre[x, y])
            for edge in (fx[x], fy[y]):
                value = value if edge is None else value * edge
            gf[x, y] = value.astype(bf)

    @pl.loop(0, 2)
    def _(i):
        for dx, y, value in squares(matrix, gf, 2 * i, 4):
            out[2 * i + dx, y] = value.astype(bf)


def call(body, counts, outs, scratch, *args):
    smem = pl.BlockSpec(memory_space=pltpu.SMEM)
    vmem = pl.BlockSpec(memory_space=pltpu.VMEM)
    return pl.pallas_call(
        functools.partial(body, counts),
        out_shape=[jax.ShapeDtypeStruct(s, d) for s, d in outs],
        in_specs=[smem] + [vmem] * (len(args) - 1),
        out_specs=[vmem] * len(outs),
        scratch_shapes=[pltpu.VMEM(s, d) for s, d in scratch],
        compiler_params=pltpu.CompilerParams(vmem_limit_bytes=48 * 1024 * 1024),
        name=body.__name__,
        cost_estimate=pl.CostEstimate(flops=400000000, bytes_accessed=2000000, transcendentals=0),
    )(*args)


def send(cells, axis, step):
    count = lax.axis_size(axis)
    pairs = [(i, i + step) for i in range(count) if 0 <= i + step < count]
    return lax.ppermute(cells, axis, pairs)


def widened(cells, axis, dim, width):
    size = cells.shape[dim]
    head = lax.slice_in_dim(cells, 0, width, axis=dim)
    tail = lax.slice_in_dim(cells, size - width, size, axis=dim)
    return send(tail, axis, 1), send(head, axis, -1)


def shards(
    volume, cotangent, conv_first, conv_second, conv_bottom, lift_weight, conv_decode, conv_final
):
    counts = (lax.axis_size("wide"), lax.axis_size("narrow"))
    pos = jnp.stack([lax.axis_index("wide"), lax.axis_index("narrow")]).astype(jnp.int32)

    def gathered(content, shift):
        groups = [
            [
                ((i + a) % counts[0]) * counts[1] + (j + b) % counts[1]
                for a in range(2)
                for b in range(2)
            ]
            for i in range(shift, counts[0] + shift, 2)
            for j in range(shift, counts[1] + shift, 2)
        ]
        return lax.all_to_all(
            content, ("wide", "narrow"), 0, 0, axis_index_groups=groups
        )

    vol = volume.transpose(1, 2, 0, 3)
    cot = cotangent.transpose(1, 2, 0, 3)
    vl, vr = widened(vol, "narrow", 1, 3)
    cl, cr = widened(cot, "narrow", 1, 2)
    vol = jnp.concatenate([vl, vol, vr], axis=1)
    cot = jnp.concatenate([cl, cot, cr], axis=1)
    vol_l, vol_r = widened(vol, "wide", 0, 3)
    cot_l, cot_r = widened(cot, "wide", 0, 2)

    matrix = ((384, 512), bf)
    full, cells = (6, 6, 32, 128), (4, 4, 32, 128)
    hid, pre, content, p2 = call(
        encode, counts,
        [(full, bf), (full, f32), ((128, 128), bf), ((4, 64, 128), bf)],
        [((10, 10, 32, 128), bf), ((8, 8, 32, 128), bf), ((8, 6, 32, 128), f32), matrix],
        pos, vol, vol_l, vol_r, forward_strips(conv_first), forward_matrix(conv_second),
    )
    four = gathered(p2, 0)
    gj, total = call(
        adjoint, counts, [(full, bf), ((64, 128), bf)], [((8, 8, 32, 128), bf), matrix],
        pos, cot, cot_l, cot_r, backward_strips(conv_final),
    )
    seg = lax.broadcasted_iota(jnp.int32, (64, 128), 1) // 32
    packed = four[0]
    for q in range(1, 4):
        packed = jnp.where(seg == q, four[q], packed)
    content = jnp.concatenate([content, total, packed], axis=0)
    early = gathered(jnp.broadcast_to(content, (4, 256, 128)), 1)
    (content,) = call(
        bottom, counts, [((4, 736, 128), bf)], [],
        pos, early, forward_matrix(conv_bottom), lift_weight,
    )
    got = gathered(content, 0)
    content, hidden = call(
        decode, counts, [((4, 256, 128), bf), ((256, 128), bf)],
        [
            ((8, 4, 64, 128), bf), ((8, 3, 64, 128), bf), ((6, 4, 32, 128), bf),
            ((6, 3, 32, 128), f32), ((6, 3, 32, 128), bf), ((4, 2, 64, 128), bf),
        ],
        pos, got, forward_matrix(conv_decode), backward_matrix(conv_decode), lift_weight.T,
    )
    got = gathered(content, 1)
    (features,) = call(
        output, counts, [(cells, bf)], [(full, bf), matrix],
        pos, hidden, hid, forward_strips(conv_final),
    )
    content, mine = call(
        deep_gradient, counts, [((4, 256, 128), bf), ((8, 64, 128), bf)], [],
        pos, got, early, backward_matrix(conv_bottom),
    )
    got = gathered(content, 0)
    (grad,) = call(
        finish, counts, [(cells, bf)], [((6, 3, 64, 128), bf), (full, bf), matrix],
        pos, got, mine, gj, pre, backward_matrix(conv_second), backward_strips(conv_first),
    )
    return features.transpose(2, 0, 1, 3), grad.transpose(2, 0, 1, 3)


def solution(mesh):
    field = P(None, "wide", "narrow", None)
    return jax.shard_map(
        shards,
        mesh=mesh,
        in_specs=(field, field) + (P(),) * 6,
        out_specs=(field, field),
        check_vma=False,
    )
```

```python
import functools

import jax
import jax.numpy as jnp
from jax import lax
from jax.experimental import pallas as pl
from jax.experimental.pallas import tpu as pltpu
from jax.sharding import PartitionSpec as P

bf = jnp.bfloat16
f32 = jnp.float32


def forward_matrix(kernel):
    chans, outs = kernel.shape[3:]
    return kernel.transpose(2, 4, 0, 1, 3).reshape(3 * outs, 9 * chans)


def backward_matrix(kernel):
    chans, outs = kernel.shape[3:]
    return jnp.flip(kernel, (0, 1, 2)).transpose(2, 3, 0, 1, 4).reshape(3 * chans, 9 * outs)


def forward_strips(kernel):
    chans, outs = kernel.shape[3:]
    return kernel.transpose(0, 2, 4, 1, 3).reshape(3, 3 * outs, 3 * chans)


def backward_strips(kernel):
    chans, outs = kernel.shape[3:]
    return jnp.flip(kernel, (0, 1, 2)).transpose(0, 2, 3, 1, 4).reshape(3, 3 * chans, 3 * outs)


def dot(a, b):
    return jnp.dot(a, b, preferred_element_type=f32)


def lanes(rows, cols=128):
    return lax.broadcasted_iota(jnp.int32, (rows, cols), 1)


def sigma(value):
    return 1.0 / (1.0 + jnp.exp(-value))


def silu(value):
    return value * sigma(value)


def slope(value):
    s = sigma(value)
    return s * (1.0 + value * (1.0 - s))


def zsum(prod, outs, span):
    pos = lanes(outs) & (span - 1)
    first, last = pos == 0, pos == span - 1
    tiles = []
    for start in range(0, prod.shape[1], 128):
        cut = slice(start, start + 128)
        below = pltpu.roll(prod[:outs, cut], 1, 1)
        above = pltpu.roll(prod[2 * outs :, cut], 127, 1)
        tiles.append(
            prod[outs : 2 * outs, cut]
            + jnp.where(first, 0.0, below)
            + jnp.where(last, 0.0, above)
        )
    return tiles


def rows_of(tiles):
    return jnp.concatenate(tiles, axis=0)


def cols_of(tiles):
    return jnp.concatenate(tiles, axis=1)


def flag(block, count):
    return jnp.where((block >= 0) & (block < count), 1.0, 0.0).astype(f32)


def selection(rows, cols, target):
    r = lax.broadcasted_iota(jnp.int32, (rows, cols), 0)
    c = lax.broadcasted_iota(jnp.int32, (rows, cols), 1)
    return jnp.where(target(r, c), 1.0, 0.0).astype(bf)


def pair_pool():
    return selection(1024, 128, lambda r, c: (r >> 9) * 64 + ((r & 127) >> 1) == c)


def pair_up():
    return selection(
        128, 256, lambda r, c: (r >> 6 == c >> 7) & ((r & 63) == (c & 127) >> 1)
    )


def block_up():
    return selection(
        128, 512, lambda r, c: (r >> 5 == c >> 7) & ((r & 31) == (c & 63) >> 1)
    )


def split(value):
    high = value.astype(bf)
    low = (value - high.astype(f32)).astype(bf)
    return rows_of([high, low])


def exact_up(value, matrix):
    rows = value.shape[0]
    out = dot(split(value), matrix)
    return out[:rows] + out[rows:]


def cross(left, right):
    low = lanes(left.shape[0]) < 64
    out = jnp.where(
        low, pltpu.roll(left.astype(f32), 64, 1), pltpu.roll(right.astype(f32), 64, 1)
    )
    return out.astype(left.dtype)


def neighbours(tiles, keep):
    chans = tiles[0].shape[0]
    seg = lanes(chans) >> 5
    masked = [t.astype(f32) * k for t, k in zip(tiles, keep)]
    cache = {}

    def rolled(q, amount):
        if (q, amount) not in cache:
            cache[q, amount] = (
                masked[q] if amount == 0 else pltpu.roll(masked[q], amount, 1)
            )
        return cache[q, amount]

    taps = []
    for dx in range(3):
        for dy in range(3):
            out = None
            for t in range(4):
                x, y = t // 2 + dx, t % 2 + dy
                q, s = (x // 2) * 2 + y // 2, (x % 2) * 2 + y % 2
                piece = rolled(q, (t - s) * 32 % 128)
                out = piece if out is None else jnp.where(seg == t, piece, out)
            taps.append(out.astype(bf))
    return rows_of(taps)


def quadrant_keep(chans, base_x, base_y, count_x, count_y):
    pos = lanes(chans)
    a, b = pos >> 6, (pos >> 5) & 1
    keep = []
    for q in range(4):
        x, y = base_x + 2 * (q // 2) + a, base_y + 2 * (q % 2) + b
        inside = (x >= 0) & (x < count_x) & (y >= 0) & (y < count_y)
        keep.append(jnp.where(inside, 1.0, 0.0).astype(f32))
    return keep


def place(pos_ref):
    return pos_ref[0], pos_ref[1]


def square_matrix(strips, out):
    blank = jnp.zeros((96, 128), bf)
    tail = jnp.zeros((96, 32), bf)
    plain = [cols_of([strips[dx], tail]) for dx in range(3)]
    moved = [pltpu.roll(t.astype(f32), 32, 1).astype(bf) for t in plain]
    for i in range(2):
        for j in range(2):
            for u in range(4):
                tile = (moved if j else plain)[u - i] if 0 <= u - i < 3 else blank
                at = 96 * (2 * i + j)
                out[at : at + 96, 128 * u : 128 * u + 128] = tile


def squares(weight, field, x, count):
    taps = [
        rows_of([field[x + u, y + v] for u in range(4) for v in range(4)])
        for y in range(0, count, 2)
    ]
    prod = dot(weight[...], cols_of(taps))
    for k in range(4):
        tiles = zsum(prod[96 * k : 96 * k + 96], 32, 128)
        for at, tile in enumerate(tiles):
            yield k // 2, 2 * at + k % 2, tile


def picked(field, x, y):
    return cols_of([field[x + i, y + j] for j in range(2) for i in range(2)])


def beside(pos, full, mine, near, far):
    rows = near.shape[0]
    full[rows : rows + 4] = mine[...]
    odd = pos[0] & 1

    @pl.when(odd == 1)
    def _():
        full[0:rows] = near[...]
        full[rows + 4 : 2 * rows + 4] = far[...]

    @pl.when(odd == 0)
    def _():
        full[0:rows] = far[...]
        full[rows + 4 : 2 * rows + 4] = near[...]


def adjoint(counts, pos, cot, cot_l, cot_r, strips, gj, total, ec, matrix):
    square_matrix(strips, matrix)
    beside(pos, ec, cot, cot_l, cot_r)

    for i in range(3):
        for dx, y, value in squares(matrix, ec, 2 * i, 6):
            gj[2 * i + dx, y] = value.astype(bf)

    sums = rows_of(
        [
            cols_of([picked(gj, 1 + 2 * x, 1), picked(gj, 1 + 2 * x, 3)])
            for x in range(2)
        ]
    )
    total[...] = dot(sums, pair_pool()).astype(bf)


def encode(
    counts, pos, vol, vol_l, vol_r, strips, second,
    hid, pre, early, p2, ev, h8, pre8, matrix,
):
    square_matrix(strips, matrix)
    w, n = place(pos)
    beside(pos, ev, vol, vol_l, vol_r)

    for i in range(4):
        for dx, y, value in squares(matrix, ev, 2 * i, 8):
            h8[2 * i + dx, y] = silu(value).astype(bf)
            if 1 <= y <= 6:
                pre8[2 * i + dx, y - 1] = value

    hid[...] = h8[1:7, 1:7]
    pre[...] = pre8[1:7]
    parts = rows_of(
        [
            cols_of([picked(h8, 2 * x, 2 * y), picked(h8, 2 * x, 2 * y + 2)])
            for x in range(4)
            for y in range(3)
        ]
    )
    pooled = dot(parts, pair_pool()) * 0.125
    low = lanes(32) < 64
    fx = [flag(w - 1, counts[0]), 1.0, 1.0, flag(w + 1, counts[0])]
    fl, fr = flag(n - 1, counts[1]), flag(n + 1, counts[1])
    fy = [jnp.where(low, fl, 1.0), jnp.ones((32, 128), f32), jnp.where(low, 1.0, fr)]
    tile = [
        [
            (pooled[(x * 3 + y) * 32 : (x * 3 + y + 1) * 32] * fy[y] * fx[x]).astype(bf)
            for y in range(3)
        ]
        for x in range(4)
    ]
    stack = [rows_of([tile[x + dx][y] for dx in range(3) for y in range(3)]) for x in range(2)]
    pre2 = zsum(dot(second[...], cols_of(stack)), 64, 64)
    spread = selection(256, 128, lambda r, c: (r & 63) >> 1 == (c & 31))
    hidden2 = cols_of([silu(v).astype(bf) for v in pre2])
    pooled2 = (dot(hidden2, spread) * 0.125).astype(bf)
    for t in range(4):
        p2[t] = pooled2
    for x in range(2):
        early[64 * x : 64 * x + 64] = pre2[x].astype(bf)


def bottom(counts, pos, got, weight, lift, out):
    w, n = place(pos)
    bx, by = 2 * ((w + 1) // 2) - 2, 2 * ((n + 1) // 2) - 2
    keep = quadrant_keep(64, bx, by, *counts)
    taps = neighbours([got[q, 192:256] for q in range(4)], keep)
    (pre,) = zsum(dot(weight[...], taps), 128, 32)
    lifted = dot(lift[...], silu(pre).astype(bf))
    up = exact_up(lifted, block_up())
    grad = slope(pre)
    ra, rb = w & 1, n & 1
    own = (1 - ra) * 2 + 1 - rb
    seg = lanes(32) >> 5
    packed = None
    for k in range(4):
        moved = pltpu.roll(grad[32 * k : 32 * k + 32], ((k - own) * 32) & 127, 1)
        packed = moved if packed is None else jnp.where(seg == k, moved, packed)
    out[512:544] = packed.astype(bf)
    for s in range(4):
        for x in range(2):
            hidden = silu(got[s, 64 * x : 64 * x + 64].astype(f32)).astype(bf)
            joined = (up[:, 128 * s : 128 * s + 128] + hidden.astype(f32)).astype(bf)
            at = (2 * s + x) * 64
            out[at : at + 64] = joined
    for r in range(3):
        row = 1 - ra + r
        for b in range(2):
            start = pl.multiple_of(128 + 32 * (row & 1), 32)
            at = 544 + 64 * r + 32 * b
            out[at : at + 32] = got[(row >> 1) * 2 + b, pl.ds(start, 32)]


def spread_quadrants(got, place_of, rows, base_x, base_y, counts, store):
    for row in range(8):
        for pair in range(4):
            q, at = (row // 4) * 2 + pair // 2, place_of(row, pair)
            if at is None:
                continue
            tile = got[q, at : at + rows]
            edge = None
            if row // 2 in (0, 3):
                edge = flag(base_x + row // 2, counts[0])
            if pair in (0, 3):
                other = flag(base_y + pair, counts[1])
                edge = other if edge is None else edge * other
            if edge is not None:
                tile = (tile.astype(f32) * edge).astype(bf)
            store(row, pair, tile)


def decode(
    counts, pos, mine, chip, side, both, weight, weight_b, lift_t, out, hidden,
    dom, mid, sums, pd, gd, gs, got,
):
    w, n = place(pos)
    ra, rb = w & 1, n & 1
    got[2 * ra + rb] = mine[...]
    got[2 * (1 - ra) + rb] = chip[...]
    got[2 * ra + 1 - rb] = side[...]
    got[2 * (1 - ra) + 1 - rb] = both[...]
    bx, by = w - ra - 1, n - rb - 1

    def put(row, pair, tile):
        dom[row, pair] = tile

    def put_sum(row, pair, tile):
        sums[row - 1, pair] = tile

    def joined_at(row, pair):
        return (((row % 4) // 2 * 2 + pair % 2) * 2 + row % 2) * 64

    def sum_at(row, pair):
        if row in (0, 7):
            return None
        return 544 + ((row - 1) % 3) * 64 + pair % 2 * 32

    spread_quadrants(got, joined_at, 64, bx, by, counts, put)
    spread_quadrants(got, sum_at, 32, bx, by, counts, put_sum)

    for row in range(8):
        for o in range(3):
            mid[row, o] = cross(dom[row, o], dom[row, o + 1])

    stack = []
    for i in range(6):
        for o in range(3):
            taps = []
            for dx in range(3):
                taps += [dom[i + dx, o], mid[i + dx, o], dom[i + dx, o + 1]]
            stack.append(rows_of(taps))
    for at, value in enumerate(zsum(dot(weight[...], cols_of(stack)), 32, 64)):
        i, o = at // 3, at % 3
        pd[i, o] = value
        total = cross(sums[i, o].astype(f32), sums[i, o + 1].astype(f32))
        gd[i, o] = (total * slope(value)).astype(bf)

    stack = []
    for j in range(4):
        for p in range(2):
            taps = []
            for dx in range(3):
                left, right = gd[j + dx, p], gd[j + dx, p + 1]
                taps += [left, cross(left, right), right]
            stack.append(rows_of(taps))
    for at, value in enumerate(zsum(dot(weight_b[...], cols_of(stack)), 64, 64)):
        gs[at // 2, at % 2] = value.astype(bf)

    parts = cols_of(
        [gs[2 * a + x, b] for a in range(2) for b in range(2) for x in range(2)]
    )
    gather = selection(1024, 128, lambda r, c: (r >> 8) * 32 + ((r & 63) >> 1) == c)
    grad_lift = dot(parts, gather).astype(bf)
    seg = lanes(32) >> 5
    packs = [got[q, 512:544].astype(f32) for q in range(4)]
    grads = []
    for k in range(4):
        grad = None
        for q in range(4):
            piece = pltpu.roll(packs[q], (q - k) * 32 % 128, 1) if q != k else packs[q]
            grad = piece if grad is None else jnp.where(seg == q, piece, grad)
        grads.append(grad)
    grad_bottom = (dot(lift_t[...], grad_lift) * rows_of(grads)).astype(bf)
    for t in range(4):
        out[t, 0:128] = grad_bottom
        for x in range(2):
            out[t, 128 + 64 * x : 192 + 64 * x] = gs[2 * ra + x, rb]
    for r in range(4):
        for o in range(2):
            at = (2 * r + o) * 32
            hidden[at : at + 32] = silu(pd[2 * ra + r, rb + o]).astype(bf)


def edges(pos, counts):
    w, n = place(pos)
    fx = [flag(w - 1, counts[0]), None, None, None, None, flag(w + 1, counts[0])]
    fy = [flag(n - 1, counts[1]), None, None, None, None, flag(n + 1, counts[1])]
    return fx, fy


def output(counts, pos, hidden, hid, strips, feat, jf, matrix):
    square_matrix(strips, matrix)
    up = dot(hidden[...], pair_up())
    fx, fy = edges(pos, counts)
    for x in range(6):
        for y in range(6):
            r, m = (x + 1) // 2, (y + 1) // 2
            at = (2 * r + m // 2) * 32
            value = up[at : at + 32, 128 * (m % 2) : 128 * (m % 2) + 128]
            value = value + hid[x, y].astype(f32)
            for edge in (fx[x], fy[y]):
                value = value if edge is None else value * edge
            jf[x, y] = value.astype(bf)

    for i in range(2):
        for dx, y, value in squares(matrix, jf, 2 * i, 4):
            feat[2 * i + dx, y] = value.astype(bf)


def deep_gradient(counts, pos, got, early, weight, out, mine):
    w, n = place(pos)
    bx, by = 2 * ((w + 1) // 2) - 2, 2 * ((n + 1) // 2) - 2
    keep = quadrant_keep(128, bx, by, *counts)
    taps = neighbours([got[q, 0:128] for q in range(4)], keep)
    (pooled,) = zsum(dot(weight[...], taps), 64, 32)
    up = exact_up(pooled * 0.125, block_up())
    for s in range(4):
        for x in range(2):
            grad = slope(early[s, 64 * x : 64 * x + 64].astype(f32))
            above = got[s, 128 + 64 * x : 192 + 64 * x].astype(f32)
            value = ((above + up[:, 128 * s : 128 * s + 128]) * grad).astype(bf)
            mine[2 * s + x] = value
    ra, rb = w & 1, n & 1
    for t in range(4):
        for k in range(2):
            a = jnp.where(ra == t // 2, k, 1 - ra)
            b = jnp.where(rb == t % 2, k, 1 - rb)
            for x in range(2):
                at = (2 * k + x) * 64
                out[t, at : at + 64] = mine[(2 * a + b) * 2 + x]


def finish(counts, pos, got, mine, gj, pre, second_b, strips, out, dom, gf, matrix):
    square_matrix(strips, matrix)
    w, n = place(pos)
    ra, rb = w & 1, n & 1

    def put(x, y, tiles):
        inside = flag(w + x - 1, counts[0]) * flag(n + y - 1, counts[1])
        for i, tile in enumerate(tiles):
            dom[2 * x + i, y] = (tile.astype(f32) * inside).astype(bf)

    far_x, far_y = 2 * (1 - ra), 2 * (1 - rb)
    part = lambda q, k: [got[q, (2 * k + i) * 64 : (2 * k + i) * 64 + 64] for i in range(2)]
    for a in range(2):
        for b in range(2):
            put(a + ra, b + rb, [mine[(2 * a + b) * 2 + i] for i in range(2)])
    for k in range(2):
        put(far_x, k + rb, part(2 * (1 - ra) + rb, k))
        put(k + ra, far_y, part(2 * ra + 1 - rb, k))
    put(far_x, far_y, part(2 * (1 - ra) + 1 - rb, 0))
    own = [[dom[row, p] for p in range(3)] for row in range(6)]
    mixed = [[cross(line[o], line[o + 1]) for o in range(2)] for line in own]
    stack = []
    for r in range(4):
        for o in range(2):
            taps = []
            for dx in range(3):
                taps += [own[r + dx][o], mixed[r + dx][o], own[r + dx][o + 1]]
            stack.append(rows_of(taps))
    grads = zsum(dot(second_b[...], cols_of(stack)), 32, 64)
    up = exact_up(rows_of(grads) * 0.125, pair_up())
    fx, fy = edges(pos, counts)
    for x in range(6):
        for y in range(6):
            r, m = (x + 1) // 2, (y + 1) // 2
            at = (2 * r + m // 2) * 32
            value = up[at : at + 32, 128 * (m % 2) : 128 * (m % 2) + 128]
            value = (value + gj[x, y].astype(f32)) * slope(pre[x, y])
            for edge in (fx[x], fy[y]):
                value = value if edge is None else value * edge
            gf[x, y] = value.astype(bf)

    for i in range(2):
        for dx, y, value in squares(matrix, gf, 2 * i, 4):
            out[2 * i + dx, y] = value.astype(bf)


def call(body, counts, outs, scratch, *args):
    smem = pl.BlockSpec(memory_space=pltpu.SMEM)
    vmem = pl.BlockSpec(memory_space=pltpu.VMEM)
    return pl.pallas_call(
        functools.partial(body, counts),
        out_shape=[jax.ShapeDtypeStruct(s, d) for s, d in outs],
        in_specs=[smem] + [vmem] * (len(args) - 1),
        out_specs=[vmem] * len(outs),
        scratch_shapes=[pltpu.VMEM(s, d) for s, d in scratch],
        compiler_params=pltpu.CompilerParams(vmem_limit_bytes=48 * 1024 * 1024),
        name=body.__name__,
        cost_estimate=pl.CostEstimate(flops=400000000, bytes_accessed=2000000, transcendentals=0),
    )(*args)


def send(cells, axis, step):
    count = lax.axis_size(axis)
    pairs = [(i, i + step) for i in range(count) if 0 <= i + step < count]
    return lax.ppermute(cells, axis, pairs)


def swap(cells, axis, shift):
    count = lax.axis_size(axis)
    lower = range(shift, count - 1, 2)
    return lax.ppermute(
        cells, axis, [(i, i + 1) for i in lower] + [(i + 1, i) for i in lower]
    )


def widened(cells, axis, dim, width):
    size = cells.shape[dim]
    head = lax.slice_in_dim(cells, 0, width, axis=dim)
    tail = lax.slice_in_dim(cells, size - width, size, axis=dim)
    return send(tail, axis, 1), send(head, axis, -1)


def shards(
    volume, cotangent, conv_first, conv_second, conv_bottom, lift_weight, conv_decode, conv_final
):
    counts = (lax.axis_size("wide"), lax.axis_size("narrow"))
    pos = jnp.stack([lax.axis_index("wide"), lax.axis_index("narrow")]).astype(jnp.int32)

    def gathered(content, shift):
        groups = [
            [
                ((i + a) % counts[0]) * counts[1] + (j + b) % counts[1]
                for a in range(2)
                for b in range(2)
            ]
            for i in range(shift, counts[0] + shift, 2)
            for j in range(shift, counts[1] + shift, 2)
        ]
        return lax.all_to_all(
            content, ("wide", "narrow"), 0, 0, axis_index_groups=groups
        )

    vol = volume.transpose(1, 2, 0, 3)
    cot = cotangent.transpose(1, 2, 0, 3)
    vl, vr = widened(vol, "narrow", 1, 3)
    cl, cr = widened(cot, "narrow", 1, 2)
    vol = jnp.concatenate([vl, vol, vr], axis=1)
    cot = jnp.concatenate([cl, cot, cr], axis=1)
    odd = pos[0] & 1

    def halves(cells, width):
        start = 4 - width
        near = lax.dynamic_slice_in_dim(cells, (1 - odd) * start, width, axis=0)
        far = lax.dynamic_slice_in_dim(cells, odd * start, width, axis=0)
        far = swap(far, "wide", 1)
        return swap(near, "wide", 0), far

    vol_l, vol_r = halves(vol, 3)
    cot_l, cot_r = halves(cot, 2)

    matrix = ((384, 512), bf)
    full, cells = (6, 6, 32, 128), (4, 4, 32, 128)
    hid, pre, content, p2 = call(
        encode, counts,
        [(full, bf), (full, f32), ((128, 128), bf), ((4, 64, 128), bf)],
        [((10, 10, 32, 128), bf), ((8, 8, 32, 128), bf), ((8, 6, 32, 128), f32), matrix],
        pos, vol, vol_l, vol_r, forward_strips(conv_first), forward_matrix(conv_second),
    )
    four = gathered(p2, 0)
    gj, total = call(
        adjoint, counts, [(full, bf), ((64, 128), bf)], [((8, 8, 32, 128), bf), matrix],
        pos, cot, cot_l, cot_r, backward_strips(conv_final),
    )
    seg = lax.broadcasted_iota(jnp.int32, (64, 128), 1) // 32
    packed = four[0]
    for q in range(1, 4):
        packed = jnp.where(seg == q, four[q], packed)
    content = jnp.concatenate([content, total, packed], axis=0)
    early = gathered(jnp.broadcast_to(content, (4, 256, 128)), 1)
    (content,) = call(
        bottom, counts, [((736, 128), bf)], [],
        pos, early, forward_matrix(conv_bottom), lift_weight,
    )
    side = swap(content, "narrow", 0)
    chip = swap(content, "wide", 0)
    both = swap(side, "wide", 0)
    content, hidden = call(
        decode, counts, [((4, 256, 128), bf), ((256, 128), bf)],
        [
            ((8, 4, 64, 128), bf), ((8, 3, 64, 128), bf), ((6, 4, 32, 128), bf),
            ((6, 3, 32, 128), f32), ((6, 3, 32, 128), bf), ((4, 2, 64, 128), bf),
            ((4, 736, 128), bf),
        ],
        pos, content, chip, side, both, forward_matrix(conv_decode), backward_matrix(conv_decode), lift_weight.T,
    )
    got = gathered(content, 1)
    (features,) = call(
        output, counts, [(cells, bf)], [(full, bf), matrix],
        pos, hidden, hid, forward_strips(conv_final),
    )
    content, mine = call(
        deep_gradient, counts, [((4, 256, 128), bf), ((8, 64, 128), bf)], [],
        pos, got, early, backward_matrix(conv_bottom),
    )
    got = gathered(content, 0)
    (grad,) = call(
        finish, counts, [(cells, bf)], [((6, 3, 64, 128), bf), (full, bf), matrix],
        pos, got, mine, gj, pre, backward_matrix(conv_second), backward_strips(conv_first),
    )
    return features.transpose(2, 0, 1, 3), grad.transpose(2, 0, 1, 3)


def solution(mesh):
    field = P(None, "wide", "narrow", None)
    return jax.shard_map(
        shards,
        mesh=mesh,
        in_specs=(field, field) + (P(),) * 6,
        out_specs=(field, field),
        check_vma=False,
    )
```

```python
import functools

import jax
import jax.numpy as jnp
from jax import lax
from jax.experimental import pallas as pl
from jax.experimental.pallas import tpu as pltpu
from jax.sharding import PartitionSpec as P


bf = jnp.bfloat16
f32 = jnp.float32


def forward_matrix(kernel):
    chans, outs = kernel.shape[3:]
    return kernel.transpose(2, 4, 0, 1, 3).reshape(3 * outs, 9 * chans)


def backward_matrix(kernel):
    chans, outs = kernel.shape[3:]
    return jnp.flip(kernel, (0, 1, 2)).transpose(2, 3, 0, 1, 4).reshape(3 * chans, 9 * outs)


def forward_strips(kernel):
    chans, outs = kernel.shape[3:]
    return kernel.transpose(0, 2, 4, 1, 3).reshape(3, 3 * outs, 3 * chans)


def backward_strips(kernel):
    chans, outs = kernel.shape[3:]
    return jnp.flip(kernel, (0, 1, 2)).transpose(0, 2, 3, 1, 4).reshape(3, 3 * chans, 3 * outs)


def dot(a, b):
    return jnp.dot(a, b, preferred_element_type=f32)


def lanes(rows, cols=128):
    return lax.broadcasted_iota(jnp.int32, (rows, cols), 1)


def sigma(value):
    return 1.0 / (1.0 + jnp.exp(-value))


def silu(value):
    return value * sigma(value)


def slope(value):
    s = sigma(value)
    return s * (1.0 + value * (1.0 - s))


def zsum(prod, outs, span):
    pos = lanes(outs) & (span - 1)
    first, last = pos == 0, pos == span - 1
    tiles = []
    for start in range(0, prod.shape[1], 128):
        cut = slice(start, start + 128)
        below = pltpu.roll(prod[:outs, cut], 1, 1)
        above = pltpu.roll(prod[2 * outs :, cut], 127, 1)
        tiles.append(
            prod[outs : 2 * outs, cut]
            + jnp.where(first, 0.0, below)
            + jnp.where(last, 0.0, above)
        )
    return tiles


def rows_of(tiles):
    return jnp.concatenate(tiles, axis=0)


def cols_of(tiles):
    return jnp.concatenate(tiles, axis=1)


def flag(block, count):
    return jnp.where((block >= 0) & (block < count), 1.0, 0.0).astype(f32)


def selection(rows, cols, target):
    r = lax.broadcasted_iota(jnp.int32, (rows, cols), 0)
    c = lax.broadcasted_iota(jnp.int32, (rows, cols), 1)
    return jnp.where(target(r, c), 1.0, 0.0).astype(bf)


def pair_pool():
    return selection(1024, 128, lambda r, c: (r >> 9) * 64 + ((r & 127) >> 1) == c)


def pair_up():
    return selection(
        128, 256, lambda r, c: (r >> 6 == c >> 7) & ((r & 63) == (c & 127) >> 1)
    )


def block_up():
    return selection(
        128, 512, lambda r, c: (r >> 5 == c >> 7) & ((r & 31) == (c & 63) >> 1)
    )


def split(value):
    high = value.astype(bf)
    low = (value - high.astype(f32)).astype(bf)
    return rows_of([high, low])


def exact_up(value, matrix):
    rows = value.shape[0]
    out = dot(split(value), matrix)
    return out[:rows] + out[rows:]


def cross(left, right):
    low = lanes(left.shape[0]) < 64
    out = jnp.where(
        low, pltpu.roll(left.astype(f32), 64, 1), pltpu.roll(right.astype(f32), 64, 1)
    )
    return out.astype(left.dtype)


def neighbours(tiles, keep):
    chans = tiles[0].shape[0]
    seg = lanes(chans) >> 5
    masked = [t.astype(f32) * k for t, k in zip(tiles, keep)]
    cache = {}

    def rolled(q, amount):
        if (q, amount) not in cache:
            cache[q, amount] = (
                masked[q] if amount == 0 else pltpu.roll(masked[q], amount, 1)
            )
        return cache[q, amount]

    taps = []
    for dx in range(3):
        for dy in range(3):
            out = None
            for t in range(4):
                x, y = t // 2 + dx, t % 2 + dy
                q, s = (x // 2) * 2 + y // 2, (x % 2) * 2 + y % 2
                piece = rolled(q, (t - s) * 32 % 128)
                out = piece if out is None else jnp.where(seg == t, piece, out)
            taps.append(out.astype(bf))
    return rows_of(taps)


def quadrant_keep(chans, base_x, base_y, count_x, count_y):
    pos = lanes(chans)
    a, b = pos >> 6, (pos >> 5) & 1
    keep = []
    for q in range(4):
        x, y = base_x + 2 * (q // 2) + a, base_y + 2 * (q % 2) + b
        inside = (x >= 0) & (x < count_x) & (y >= 0) & (y < count_y)
        keep.append(jnp.where(inside, 1.0, 0.0).astype(f32))
    return keep


def place(pos_ref):
    return pos_ref[0], pos_ref[1]


def square_matrix(strips, out):
    blank = jnp.zeros((96, 128), bf)
    tail = jnp.zeros((96, 32), bf)
    plain = [cols_of([strips[dx], tail]) for dx in range(3)]
    moved = [pltpu.roll(t.astype(f32), 32, 1).astype(bf) for t in plain]
    for i in range(2):
        for j in range(2):
            for u in range(4):
                tile = (moved if j else plain)[u - i] if 0 <= u - i < 3 else blank
                at = 96 * (2 * i + j)
                out[at : at + 96, 128 * u : 128 * u + 128] = tile


def squares(weight, field, x, count):
    taps = [
        rows_of([field[x + u, y + v] for u in range(4) for v in range(4)])
        for y in range(0, count, 2)
    ]
    prod = dot(weight[...], cols_of(taps))
    for k in range(4):
        tiles = zsum(prod[96 * k : 96 * k + 96], 32, 128)
        for at, tile in enumerate(tiles):
            yield k // 2, 2 * at + k % 2, tile


def picked(field, x, y):
    return cols_of([field[x + i, y + j] for j in range(2) for i in range(2)])


def beside(pos, full, mine, close, start, far):
    rows, wide = far.shape[:2]
    near = close[start : start + rows * wide].reshape(far.shape)
    full[rows : rows + 4] = mine[...]
    odd = pos[0] & 1

    @pl.when(odd == 1)
    def _():
        full[0:rows] = near
        full[rows + 4 : 2 * rows + 4] = far[...]

    @pl.when(odd == 0)
    def _():
        full[0:rows] = far[...]
        full[rows + 4 : 2 * rows + 4] = near


def adjoint(counts, pos, cot, close, far, strips, gj, total, ec, matrix):
    square_matrix(strips, matrix)
    beside(pos, ec, cot, close, 30, far)

    for i in range(3):
        for dx, y, value in squares(matrix, ec, 2 * i, 6):
            gj[2 * i + dx, y] = value.astype(bf)

    sums = rows_of(
        [
            cols_of([picked(gj, 1 + 2 * x, 1), picked(gj, 1 + 2 * x, 3)])
            for x in range(2)
        ]
    )
    total[...] = dot(sums, pair_pool()).astype(bf)


def encode(
    counts, pos, vol, close, far, strips, second,
    hid, pre, early, p2, ev, h8, pre8, matrix,
):
    square_matrix(strips, matrix)
    w, n = place(pos)
    beside(pos, ev, vol, close, 0, far)

    for i in range(4):
        for dx, y, value in squares(matrix, ev, 2 * i, 8):
            h8[2 * i + dx, y] = silu(value).astype(bf)
            if 1 <= y <= 6:
                pre8[2 * i + dx, y - 1] = value

    hid[...] = h8[1:7, 1:7]
    pre[...] = pre8[1:7]
    parts = rows_of(
        [
            cols_of([picked(h8, 2 * x, 2 * y), picked(h8, 2 * x, 2 * y + 2)])
            for x in range(4)
            for y in range(3)
        ]
    )
    pooled = dot(parts, pair_pool()) * 0.125
    low = lanes(32) < 64
    fx = [flag(w - 1, counts[0]), 1.0, 1.0, flag(w + 1, counts[0])]
    fl, fr = flag(n - 1, counts[1]), flag(n + 1, counts[1])
    fy = [jnp.where(low, fl, 1.0), jnp.ones((32, 128), f32), jnp.where(low, 1.0, fr)]
    tile = [
        [
            (pooled[(x * 3 + y) * 32 : (x * 3 + y + 1) * 32] * fy[y] * fx[x]).astype(bf)
            for y in range(3)
        ]
        for x in range(4)
    ]
    stack = [rows_of([tile[x + dx][y] for dx in range(3) for y in range(3)]) for x in range(2)]
    pre2 = zsum(dot(second[...], cols_of(stack)), 64, 64)
    spread = selection(256, 128, lambda r, c: (r & 63) >> 1 == (c & 31))
    hidden2 = cols_of([silu(v).astype(bf) for v in pre2])
    pooled2 = (dot(hidden2, spread) * 0.125).astype(bf)
    for t in range(4):
        p2[t] = pooled2
    for x in range(2):
        early[64 * x : 64 * x + 64] = pre2[x].astype(bf)


def bottom(counts, pos, got, weight, lift, out):
    w, n = place(pos)
    bx, by = 2 * ((w + 1) // 2) - 2, 2 * ((n + 1) // 2) - 2
    keep = quadrant_keep(64, bx, by, *counts)
    taps = neighbours([got[q, 192:256] for q in range(4)], keep)
    (pre,) = zsum(dot(weight[...], taps), 128, 32)
    lifted = dot(lift[...], silu(pre).astype(bf))
    up = exact_up(lifted, block_up())
    grad = slope(pre)
    ra, rb = w & 1, n & 1
    own = (1 - ra) * 2 + 1 - rb
    seg = lanes(32) >> 5
    packed = None
    for k in range(4):
        moved = pltpu.roll(grad[32 * k : 32 * k + 32], ((k - own) * 32) & 127, 1)
        packed = moved if packed is None else jnp.where(seg == k, moved, packed)
    out[512:544] = packed.astype(bf)
    for s in range(4):
        for x in range(2):
            hidden = silu(got[s, 64 * x : 64 * x + 64].astype(f32)).astype(bf)
            joined = (up[:, 128 * s : 128 * s + 128] + hidden.astype(f32)).astype(bf)
            at = (2 * s + x) * 64
            out[at : at + 64] = joined
    for r in range(3):
        row = 1 - ra + r
        for b in range(2):
            start = pl.multiple_of(128 + 32 * (row & 1), 32)
            at = 544 + 64 * r + 32 * b
            out[at : at + 32] = got[(row >> 1) * 2 + b, pl.ds(start, 32)]


def spread_quadrants(got, place_of, rows, base_x, base_y, counts, store):
    for row in range(8):
        for pair in range(4):
            q, at = (row // 4) * 2 + pair // 2, place_of(row, pair)
            if at is None:
                continue
            tile = got[q, at : at + rows]
            edge = None
            if row // 2 in (0, 3):
                edge = flag(base_x + row // 2, counts[0])
            if pair in (0, 3):
                other = flag(base_y + pair, counts[1])
                edge = other if edge is None else edge * other
            if edge is not None:
                tile = (tile.astype(f32) * edge).astype(bf)
            store(row, pair, tile)


def decode(
    counts, pos, mine, chip, side, both, weight, weight_b, lift_t, out, hidden,
    dom, mid, sums, pd, gd, gs, got,
):
    w, n = place(pos)
    ra, rb = w & 1, n & 1
    got[2 * ra + rb] = mine[...]
    got[2 * (1 - ra) + rb] = chip[...]
    got[2 * ra + 1 - rb] = side[...]
    got[2 * (1 - ra) + 1 - rb] = both[...]
    bx, by = w - ra - 1, n - rb - 1

    def put(row, pair, tile):
        dom[row, pair] = tile

    def put_sum(row, pair, tile):
        sums[row - 1, pair] = tile

    def joined_at(row, pair):
        return (((row % 4) // 2 * 2 + pair % 2) * 2 + row % 2) * 64

    def sum_at(row, pair):
        if row in (0, 7):
            return None
        return 544 + ((row - 1) % 3) * 64 + pair % 2 * 32

    spread_quadrants(got, joined_at, 64, bx, by, counts, put)
    spread_quadrants(got, sum_at, 32, bx, by, counts, put_sum)

    for row in range(8):
        for o in range(3):
            mid[row, o] = cross(dom[row, o], dom[row, o + 1])

    stack = []
    for i in range(6):
        for o in range(3):
            taps = []
            for dx in range(3):
                taps += [dom[i + dx, o], mid[i + dx, o], dom[i + dx, o + 1]]
            stack.append(rows_of(taps))
    for at, value in enumerate(zsum(dot(weight[...], cols_of(stack)), 32, 64)):
        i, o = at // 3, at % 3
        pd[i, o] = value
        total = cross(sums[i, o].astype(f32), sums[i, o + 1].astype(f32))
        gd[i, o] = (total * slope(value)).astype(bf)

    stack = []
    for j in range(4):
        for p in range(2):
            taps = []
            for dx in range(3):
                left, right = gd[j + dx, p], gd[j + dx, p + 1]
                taps += [left, cross(left, right), right]
            stack.append(rows_of(taps))
    for at, value in enumerate(zsum(dot(weight_b[...], cols_of(stack)), 64, 64)):
        gs[at // 2, at % 2] = value.astype(bf)

    parts = cols_of(
        [gs[2 * a + x, b] for a in range(2) for b in range(2) for x in range(2)]
    )
    gather = selection(1024, 128, lambda r, c: (r >> 8) * 32 + ((r & 63) >> 1) == c)
    grad_lift = dot(parts, gather).astype(bf)
    seg = lanes(32) >> 5
    packs = [got[q, 512:544].astype(f32) for q in range(4)]
    grads = []
    for k in range(4):
        grad = None
        for q in range(4):
            piece = pltpu.roll(packs[q], (q - k) * 32 % 128, 1) if q != k else packs[q]
            grad = piece if grad is None else jnp.where(seg == q, piece, grad)
        grads.append(grad)
    grad_bottom = (dot(lift_t[...], grad_lift) * rows_of(grads)).astype(bf)
    for t in range(4):
        out[t, 0:128] = grad_bottom
        for x in range(2):
            out[t, 128 + 64 * x : 192 + 64 * x] = gs[2 * ra + x, rb]
    for r in range(4):
        for o in range(2):
            at = (2 * r + o) * 32
            hidden[at : at + 32] = silu(pd[2 * ra + r, rb + o]).astype(bf)


def edges(pos, counts):
    w, n = place(pos)
    fx = [flag(w - 1, counts[0]), None, None, None, None, flag(w + 1, counts[0])]
    fy = [flag(n - 1, counts[1]), None, None, None, None, flag(n + 1, counts[1])]
    return fx, fy


def output(counts, pos, hidden, hid, strips, feat, jf, matrix):
    square_matrix(strips, matrix)
    up = dot(hidden[...], pair_up())
    fx, fy = edges(pos, counts)
    for x in range(6):
        for y in range(6):
            r, m = (x + 1) // 2, (y + 1) // 2
            at = (2 * r + m // 2) * 32
            value = up[at : at + 32, 128 * (m % 2) : 128 * (m % 2) + 128]
            value = value + hid[x, y].astype(f32)
            for edge in (fx[x], fy[y]):
                value = value if edge is None else value * edge
            jf[x, y] = value.astype(bf)

    for i in range(2):
        for dx, y, value in squares(matrix, jf, 2 * i, 4):
            feat[2 * i + dx, y] = value.astype(bf)


def deep_gradient(counts, pos, got, early, weight, out, mine):
    w, n = place(pos)
    bx, by = 2 * ((w + 1) // 2) - 2, 2 * ((n + 1) // 2) - 2
    keep = quadrant_keep(128, bx, by, *counts)
    taps = neighbours([got[q, 0:128] for q in range(4)], keep)
    (pooled,) = zsum(dot(weight[...], taps), 64, 32)
    up = exact_up(pooled * 0.125, block_up())
    for s in range(4):
        for x in range(2):
            grad = slope(early[s, 64 * x : 64 * x + 64].astype(f32))
            above = got[s, 128 + 64 * x : 192 + 64 * x].astype(f32)
            value = ((above + up[:, 128 * s : 128 * s + 128]) * grad).astype(bf)
            mine[2 * s + x] = value
    ra, rb = w & 1, n & 1
    for t in range(4):
        for k in range(2):
            a = jnp.where(ra == t // 2, k, 1 - ra)
            b = jnp.where(rb == t % 2, k, 1 - rb)
            for x in range(2):
                at = (2 * k + x) * 64
                out[t, at : at + 64] = mine[(2 * a + b) * 2 + x]


def finish(counts, pos, got, mine, gj, pre, second_b, strips, out, dom, gf, matrix):
    square_matrix(strips, matrix)
    w, n = place(pos)
    ra, rb = w & 1, n & 1

    def put(x, y, tiles):
        inside = flag(w + x - 1, counts[0]) * flag(n + y - 1, counts[1])
        for i, tile in enumerate(tiles):
            dom[2 * x + i, y] = (tile.astype(f32) * inside).astype(bf)

    far_x, far_y = 2 * (1 - ra), 2 * (1 - rb)
    part = lambda q, k: [got[q, (2 * k + i) * 64 : (2 * k + i) * 64 + 64] for i in range(2)]
    for a in range(2):
        for b in range(2):
            put(a + ra, b + rb, [mine[(2 * a + b) * 2 + i] for i in range(2)])
    for k in range(2):
        put(far_x, k + rb, part(2 * (1 - ra) + rb, k))
        put(k + ra, far_y, part(2 * ra + 1 - rb, k))
    put(far_x, far_y, part(2 * (1 - ra) + 1 - rb, 0))
    own = [[dom[row, p] for p in range(3)] for row in range(6)]
    mixed = [[cross(line[o], line[o + 1]) for o in range(2)] for line in own]
    stack = []
    for r in range(4):
        for o in range(2):
            taps = []
            for dx in range(3):
                taps += [own[r + dx][o], mixed[r + dx][o], own[r + dx][o + 1]]
            stack.append(rows_of(taps))
    grads = zsum(dot(second_b[...], cols_of(stack)), 32, 64)
    up = exact_up(rows_of(grads) * 0.125, pair_up())
    fx, fy = edges(pos, counts)
    for x in range(6):
        for y in range(6):
            r, m = (x + 1) // 2, (y + 1) // 2
            at = (2 * r + m // 2) * 32
            value = up[at : at + 32, 128 * (m % 2) : 128 * (m % 2) + 128]
            value = (value + gj[x, y].astype(f32)) * slope(pre[x, y])
            for edge in (fx[x], fy[y]):
                value = value if edge is None else value * edge
            gf[x, y] = value.astype(bf)

    for i in range(2):
        for dx, y, value in squares(matrix, gf, 2 * i, 4):
            out[2 * i + dx, y] = value.astype(bf)


def call(body, counts, outs, scratch, *args):
    smem = pl.BlockSpec(memory_space=pltpu.SMEM)
    vmem = pl.BlockSpec(memory_space=pltpu.VMEM)
    return pl.pallas_call(
        functools.partial(body, counts),
        out_shape=[jax.ShapeDtypeStruct(s, d) for s, d in outs],
        in_specs=[smem] + [vmem] * (len(args) - 1),
        out_specs=[vmem] * len(outs),
        scratch_shapes=[pltpu.VMEM(s, d) for s, d in scratch],
        compiler_params=pltpu.CompilerParams(vmem_limit_bytes=48 * 1024 * 1024),
        cost_estimate=pl.CostEstimate(flops=400000000, bytes_accessed=2000000, transcendentals=0),
    )(*args)


def send(cells, axis, step):
    count = lax.axis_size(axis)
    pairs = [(i, i + step) for i in range(count) if 0 <= i + step < count]
    return lax.ppermute(cells, axis, pairs)


def swap(cells, axis, shift):
    count = lax.axis_size(axis)
    lower = range(shift, count - 1, 2)
    return lax.ppermute(
        cells, axis, [(i, i + 1) for i in lower] + [(i + 1, i) for i in lower]
    )


def shards(
    volume, cotangent, conv_first, conv_second, conv_bottom, lift_weight, conv_decode, conv_final
):
    counts = (lax.axis_size("wide"), lax.axis_size("narrow"))
    pos = jnp.stack([lax.axis_index("wide"), lax.axis_index("narrow")]).astype(jnp.int32)

    def gathered(content, shift):
        groups = [
            [
                ((i + a) % counts[0]) * counts[1] + (j + b) % counts[1]
                for a in range(2)
                for b in range(2)
            ]
            for i in range(shift, counts[0] + shift, 2)
            for j in range(shift, counts[1] + shift, 2)
        ]
        return lax.all_to_all(
            content, ("wide", "narrow"), 0, 0, axis_index_groups=groups
        )

    vol = volume.transpose(1, 2, 0, 3)
    cot = cotangent.transpose(1, 2, 0, 3)
    low = send(jnp.concatenate([vol[:, 1:], cot[:, 2:]], axis=1), "narrow", 1)
    high = send(jnp.concatenate([vol[:, :3], cot[:, :2]], axis=1), "narrow", -1)
    vol = jnp.concatenate([low[:, :3], vol, high[:, :3]], axis=1)
    cot = jnp.concatenate([low[:, 3:], cot, high[:, 3:]], axis=1)
    odd = pos[0] & 1

    def edge(cells, width, side):
        return lax.dynamic_slice_in_dim(cells, side * (4 - width), width, axis=0)

    vol_far = swap(edge(vol, 3, odd), "wide", 1)
    flat = lambda cells: cells.reshape(-1, 32, 128)
    near = [flat(edge(vol, 3, 1 - odd)), flat(edge(cot, 2, 1 - odd))]
    near = swap(jnp.concatenate(near, axis=0), "wide", 0)
    cot_far = swap(edge(cot, 2, odd), "wide", 1)

    matrix = ((384, 512), bf)
    full, cells = (6, 6, 32, 128), (4, 4, 32, 128)
    hid, pre, content, p2 = call(
        encode, counts,
        [(full, bf), (full, f32), ((128, 128), bf), ((4, 64, 128), bf)],
        [((10, 10, 32, 128), bf), ((8, 8, 32, 128), bf), ((8, 6, 32, 128), f32), matrix],
        pos, vol, near, vol_far, forward_strips(conv_first), forward_matrix(conv_second),
    )
    four = gathered(p2, 0)
    gj, total = call(
        adjoint, counts, [(full, bf), ((64, 128), bf)], [((8, 8, 32, 128), bf), matrix],
        pos, cot, near, cot_far, backward_strips(conv_final),
    )
    seg = lax.broadcasted_iota(jnp.int32, (64, 128), 1) // 32
    packed = four[0]
    for q in range(1, 4):
        packed = jnp.where(seg == q, four[q], packed)
    content = jnp.concatenate([content, total, packed], axis=0)
    early = gathered(jnp.broadcast_to(content, (4, 256, 128)), 1)
    (content,) = call(
        bottom, counts, [((736, 128), bf)], [],
        pos, early, forward_matrix(conv_bottom), lift_weight,
    )
    side = swap(content, "narrow", 0)
    chip = swap(content, "wide", 0)
    both = swap(side, "wide", 0)
    content, hidden = call(
        decode, counts, [((4, 256, 128), bf), ((256, 128), bf)],
        [
            ((8, 4, 64, 128), bf), ((8, 3, 64, 128), bf), ((6, 4, 32, 128), bf),
            ((6, 3, 32, 128), f32), ((6, 3, 32, 128), bf), ((4, 2, 64, 128), bf),
            ((4, 736, 128), bf),
        ],
        pos, content, chip, side, both, forward_matrix(conv_decode), backward_matrix(conv_decode), lift_weight.T,
    )
    got = gathered(content, 1)
    (features,) = call(
        output, counts, [(cells, bf)], [(full, bf), matrix],
        pos, hidden, hid, forward_strips(conv_final),
    )
    content, mine = call(
        deep_gradient, counts, [((4, 256, 128), bf), ((8, 64, 128), bf)], [],
        pos, got, early, backward_matrix(conv_bottom),
    )
    got = gathered(content, 0)
    (grad,) = call(
        finish, counts, [(cells, bf)], [((6, 3, 64, 128), bf), (full, bf), matrix],
        pos, got, mine, gj, pre, backward_matrix(conv_second), backward_strips(conv_first),
    )
    return features.transpose(2, 0, 1, 3), grad.transpose(2, 0, 1, 3)


def solution(mesh):
    field = P(None, "wide", "narrow", None)

    return jax.shard_map(
        shards,
        mesh=mesh,
        in_specs=(field, field) + (P(),) * 6,
        out_specs=(field, field),
        check_vma=False,
    )
```

```python
import functools

import jax
import jax.numpy as jnp
from jax import lax
from jax.experimental import pallas as pl
from jax.experimental.pallas import tpu as pltpu
from jax.sharding import PartitionSpec as P


bf = jnp.bfloat16
f32 = jnp.float32


def forward_matrix(kernel):
    chans, outs = kernel.shape[3:]
    return kernel.transpose(2, 4, 0, 1, 3).reshape(3 * outs, 9 * chans)


def backward_matrix(kernel):
    chans, outs = kernel.shape[3:]
    return jnp.flip(kernel, (0, 1, 2)).transpose(2, 3, 0, 1, 4).reshape(3 * chans, 9 * outs)


def forward_strips(kernel):
    chans, outs = kernel.shape[3:]
    return kernel.transpose(0, 2, 4, 1, 3).reshape(3, 3 * outs, 3 * chans)


def backward_strips(kernel):
    chans, outs = kernel.shape[3:]
    return jnp.flip(kernel, (0, 1, 2)).transpose(0, 2, 3, 1, 4).reshape(3, 3 * chans, 3 * outs)


def dot(a, b):
    return jnp.dot(a, b, preferred_element_type=f32)


def lanes(rows, cols=128):
    return lax.broadcasted_iota(jnp.int32, (rows, cols), 1)


def sigma(value):
    return 1.0 / (1.0 + jnp.exp(-value))


def silu(value):
    return value * sigma(value)


def slope(value):
    s = sigma(value)
    return s * (1.0 + value * (1.0 - s))


def zsum(prod, outs, span):
    pos = lanes(outs) & (span - 1)
    first, last = pos == 0, pos == span - 1
    tiles = []
    for start in range(0, prod.shape[1], 128):
        cut = slice(start, start + 128)
        below = pltpu.roll(prod[:outs, cut], 1, 1)
        above = pltpu.roll(prod[2 * outs :, cut], 127, 1)
        tiles.append(
            prod[outs : 2 * outs, cut]
            + jnp.where(first, 0.0, below)
            + jnp.where(last, 0.0, above)
        )
    return tiles


def rows_of(tiles):
    return jnp.concatenate(tiles, axis=0)


def cols_of(tiles):
    return jnp.concatenate(tiles, axis=1)


def flag(block, count):
    return jnp.where((block >= 0) & (block < count), 1.0, 0.0).astype(f32)


def selection(rows, cols, target):
    r = lax.broadcasted_iota(jnp.int32, (rows, cols), 0)
    c = lax.broadcasted_iota(jnp.int32, (rows, cols), 1)
    return jnp.where(target(r, c), 1.0, 0.0).astype(bf)


def pair_pool():
    return selection(1024, 128, lambda r, c: (r >> 9) * 64 + ((r & 127) >> 1) == c)


def pair_up():
    return selection(
        128, 256, lambda r, c: (r >> 6 == c >> 7) & ((r & 63) == (c & 127) >> 1)
    )


def block_up():
    return selection(
        128, 512, lambda r, c: (r >> 5 == c >> 7) & ((r & 31) == (c & 63) >> 1)
    )


def split(value):
    high = value.astype(bf)
    low = (value - high.astype(f32)).astype(bf)
    return rows_of([high, low])


def exact_up(value, matrix):
    rows = value.shape[0]
    out = dot(split(value), matrix)
    return out[:rows] + out[rows:]


def cross(left, right):
    low = lanes(left.shape[0]) < 64
    out = jnp.where(
        low, pltpu.roll(left.astype(f32), 64, 1), pltpu.roll(right.astype(f32), 64, 1)
    )
    return out.astype(left.dtype)


def neighbours(tiles, keep):
    chans = tiles[0].shape[0]
    seg = lanes(chans) >> 5
    masked = [t.astype(f32) * k for t, k in zip(tiles, keep)]
    cache = {}

    def rolled(q, amount):
        if (q, amount) not in cache:
            cache[q, amount] = (
                masked[q] if amount == 0 else pltpu.roll(masked[q], amount, 1)
            )
        return cache[q, amount]

    taps = []
    for dx in range(3):
        for dy in range(3):
            out = None
            for t in range(4):
                x, y = t // 2 + dx, t % 2 + dy
                q, s = (x // 2) * 2 + y // 2, (x % 2) * 2 + y % 2
                piece = rolled(q, (t - s) * 32 % 128)
                out = piece if out is None else jnp.where(seg == t, piece, out)
            taps.append(out.astype(bf))
    return rows_of(taps)


def quadrant_keep(chans, base_x, base_y, count_x, count_y):
    pos = lanes(chans)
    a, b = pos >> 6, (pos >> 5) & 1
    keep = []
    for q in range(4):
        x, y = base_x + 2 * (q // 2) + a, base_y + 2 * (q % 2) + b
        inside = (x >= 0) & (x < count_x) & (y >= 0) & (y < count_y)
        keep.append(jnp.where(inside, 1.0, 0.0).astype(f32))
    return keep


def place(pos_ref):
    return pos_ref[0], pos_ref[1]


def square_matrix(strips, out):
    blank = jnp.zeros((96, 128), bf)
    tail = jnp.zeros((96, 32), bf)
    plain = [cols_of([strips[dx], tail]) for dx in range(3)]
    moved = [pltpu.roll(t.astype(f32), 32, 1).astype(bf) for t in plain]
    for i in range(2):
        for j in range(2):
            for u in range(4):
                tile = (moved if j else plain)[u - i] if 0 <= u - i < 3 else blank
                at = 96 * (2 * i + j)
                out[at : at + 96, 128 * u : 128 * u + 128] = tile


def squares(weight, field, x, count):
    taps = [
        rows_of([field[x + u, y + v] for u in range(4) for v in range(4)])
        for y in range(0, count, 2)
    ]
    prod = dot(weight[...], cols_of(taps))
    for k in range(4):
        tiles = zsum(prod[96 * k : 96 * k + 96], 32, 128)
        for at, tile in enumerate(tiles):
            yield k // 2, 2 * at + k % 2, tile


def picked(field, x, y):
    return cols_of([field[x + i, y + j] for j in range(2) for i in range(2)])


def beside(pos, full, mine, close, start, far):
    rows, wide = far.shape[:2]
    near = close[start : start + rows * wide].reshape(far.shape)
    full[rows : rows + 4] = mine[...]
    odd = pos[0] & 1

    @pl.when(odd == 1)
    def _():
        full[0:rows] = near
        full[rows + 4 : 2 * rows + 4] = far[...]

    @pl.when(odd == 0)
    def _():
        full[0:rows] = far[...]
        full[rows + 4 : 2 * rows + 4] = near


def adjoint(counts, pos, cot, close, far, strips, gj, total, ec, matrix):
    square_matrix(strips, matrix)
    beside(pos, ec, cot, close, 30, far)

    for i in range(3):
        for dx, y, value in squares(matrix, ec, 2 * i, 6):
            gj[2 * i + dx, y] = value.astype(bf)

    sums = rows_of(
        [
            cols_of([picked(gj, 1 + 2 * x, 1), picked(gj, 1 + 2 * x, 3)])
            for x in range(2)
        ]
    )
    total[...] = dot(sums, pair_pool()).astype(bf)


def encode(
    counts, pos, vol, close, far, strips, second,
    hid, pre, early, p2, ev, h8, pre8, matrix,
):
    square_matrix(strips, matrix)
    w, n = place(pos)
    beside(pos, ev, vol, close, 0, far)

    for i in range(4):
        for dx, y, value in squares(matrix, ev, 2 * i, 8):
            h8[2 * i + dx, y] = silu(value).astype(bf)
            if 1 <= y <= 6:
                pre8[2 * i + dx, y - 1] = value

    hid[...] = h8[1:7, 1:7]
    pre[...] = pre8[1:7]
    parts = rows_of(
        [
            cols_of([picked(h8, 2 * x, 2 * y), picked(h8, 2 * x, 2 * y + 2)])
            for x in range(4)
            for y in range(3)
        ]
    )
    pooled = dot(parts, pair_pool()) * 0.125
    low = lanes(32) < 64
    fx = [flag(w - 1, counts[0]), 1.0, 1.0, flag(w + 1, counts[0])]
    fl, fr = flag(n - 1, counts[1]), flag(n + 1, counts[1])
    fy = [jnp.where(low, fl, 1.0), jnp.ones((32, 128), f32), jnp.where(low, 1.0, fr)]
    tile = [
        [
            (pooled[(x * 3 + y) * 32 : (x * 3 + y + 1) * 32] * fy[y] * fx[x]).astype(bf)
            for y in range(3)
        ]
        for x in range(4)
    ]
    stack = [rows_of([tile[x + dx][y] for dx in range(3) for y in range(3)]) for x in range(2)]
    pre2 = zsum(dot(second[...], cols_of(stack)), 64, 64)
    spread = selection(256, 128, lambda r, c: (r & 63) >> 1 == (c & 31))
    hidden2 = cols_of([silu(v).astype(bf) for v in pre2])
    pooled2 = (dot(hidden2, spread) * 0.125).astype(bf)
    for t in range(4):
        p2[t] = pooled2
    for x in range(2):
        early[64 * x : 64 * x + 64] = pre2[x].astype(bf)


def bottom(counts, pos, got, weight, lift, out):
    w, n = place(pos)
    bx, by = 2 * ((w + 1) // 2) - 2, 2 * ((n + 1) // 2) - 2
    keep = quadrant_keep(64, bx, by, *counts)
    taps = neighbours([got[q, 192:256] for q in range(4)], keep)
    (pre,) = zsum(dot(weight[...], taps), 128, 32)
    lifted = dot(lift[...], silu(pre).astype(bf))
    up = exact_up(lifted, block_up())
    grad = slope(pre)
    ra, rb = w & 1, n & 1
    own = (1 - ra) * 2 + 1 - rb
    seg = lanes(32) >> 5
    packed = None
    for k in range(4):
        moved = pltpu.roll(grad[32 * k : 32 * k + 32], ((k - own) * 32) & 127, 1)
        packed = moved if packed is None else jnp.where(seg == k, moved, packed)
    out[512:544] = packed.astype(bf)
    for s in range(4):
        for x in range(2):
            hidden = silu(got[s, 64 * x : 64 * x + 64].astype(f32)).astype(bf)
            joined = (up[:, 128 * s : 128 * s + 128] + hidden.astype(f32)).astype(bf)
            at = (2 * s + x) * 64
            out[at : at + 64] = joined
    for r in range(3):
        row = 1 - ra + r
        for b in range(2):
            start = pl.multiple_of(128 + 32 * (row & 1), 32)
            at = 544 + 64 * r + 32 * b
            out[at : at + 32] = got[(row >> 1) * 2 + b, pl.ds(start, 32)]


def spread_quadrants(got, place_of, rows, base_x, base_y, counts, store):
    for row in range(8):
        for pair in range(4):
            q, at = (row // 4) * 2 + pair // 2, place_of(row, pair)
            if at is None:
                continue
            tile = got[q, at : at + rows]
            edge = None
            if row // 2 in (0, 3):
                edge = flag(base_x + row // 2, counts[0])
            if pair in (0, 3):
                other = flag(base_y + pair, counts[1])
                edge = other if edge is None else edge * other
            if edge is not None:
                tile = (tile.astype(f32) * edge).astype(bf)
            store(row, pair, tile)


def decode(
    counts, pos, mine, chip, side, both, weight, weight_b, lift_t, out, hidden,
    dom, mid, sums, pd, gd, gs, got,
):
    w, n = place(pos)
    ra, rb = w & 1, n & 1
    got[2 * ra + rb] = mine[...]
    got[2 * (1 - ra) + rb] = chip[...]
    got[2 * ra + 1 - rb] = side[...]
    got[2 * (1 - ra) + 1 - rb] = both[...]
    bx, by = w - ra - 1, n - rb - 1

    def put(row, pair, tile):
        dom[row, pair] = tile

    def put_sum(row, pair, tile):
        sums[row - 1, pair] = tile

    def joined_at(row, pair):
        return (((row % 4) // 2 * 2 + pair % 2) * 2 + row % 2) * 64

    def sum_at(row, pair):
        if row in (0, 7):
            return None
        return 544 + ((row - 1) % 3) * 64 + pair % 2 * 32

    spread_quadrants(got, joined_at, 64, bx, by, counts, put)
    spread_quadrants(got, sum_at, 32, bx, by, counts, put_sum)

    for row in range(8):
        for o in range(3):
            mid[row, o] = cross(dom[row, o], dom[row, o + 1])

    stack = []
    for i in range(6):
        for o in range(3):
            taps = []
            for dx in range(3):
                taps += [dom[i + dx, o], mid[i + dx, o], dom[i + dx, o + 1]]
            stack.append(rows_of(taps))
    for at, value in enumerate(zsum(dot(weight[...], cols_of(stack)), 32, 64)):
        i, o = at // 3, at % 3
        pd[i, o] = value
        total = cross(sums[i, o].astype(f32), sums[i, o + 1].astype(f32))
        gd[i, o] = (total * slope(value)).astype(bf)

    stack = []
    for j in range(4):
        for p in range(2):
            taps = []
            for dx in range(3):
                left, right = gd[j + dx, p], gd[j + dx, p + 1]
                taps += [left, cross(left, right), right]
            stack.append(rows_of(taps))
    for at, value in enumerate(zsum(dot(weight_b[...], cols_of(stack)), 64, 64)):
        gs[at // 2, at % 2] = value.astype(bf)

    parts = cols_of(
        [gs[2 * a + x, b] for a in range(2) for b in range(2) for x in range(2)]
    )
    gather = selection(1024, 128, lambda r, c: (r >> 8) * 32 + ((r & 63) >> 1) == c)
    grad_lift = dot(parts, gather).astype(bf)
    seg = lanes(32) >> 5
    packs = [got[q, 512:544].astype(f32) for q in range(4)]
    grads = []
    for k in range(4):
        grad = None
        for q in range(4):
            piece = pltpu.roll(packs[q], (q - k) * 32 % 128, 1) if q != k else packs[q]
            grad = piece if grad is None else jnp.where(seg == q, piece, grad)
        grads.append(grad)
    grad_bottom = (dot(lift_t[...], grad_lift) * rows_of(grads)).astype(bf)
    for t in range(4):
        out[t, 0:128] = grad_bottom
        for x in range(2):
            out[t, 128 + 64 * x : 192 + 64 * x] = gs[2 * ra + x, rb]
    for r in range(4):
        for o in range(2):
            at = (2 * r + o) * 32
            hidden[at : at + 32] = silu(pd[2 * ra + r, rb + o]).astype(bf)


def edges(pos, counts):
    w, n = place(pos)
    fx = [flag(w - 1, counts[0]), None, None, None, None, flag(w + 1, counts[0])]
    fy = [flag(n - 1, counts[1]), None, None, None, None, flag(n + 1, counts[1])]
    return fx, fy


def output(counts, pos, hidden, hid, strips, feat, jf, matrix):
    square_matrix(strips, matrix)
    up = dot(hidden[...], pair_up())
    fx, fy = edges(pos, counts)
    for x in range(6):
        for y in range(6):
            r, m = (x + 1) // 2, (y + 1) // 2
            at = (2 * r + m // 2) * 32
            value = up[at : at + 32, 128 * (m % 2) : 128 * (m % 2) + 128]
            value = value + hid[x, y].astype(f32)
            for edge in (fx[x], fy[y]):
                value = value if edge is None else value * edge
            jf[x, y] = value.astype(bf)

    for i in range(2):
        for dx, y, value in squares(matrix, jf, 2 * i, 4):
            feat[2 * i + dx, y] = value.astype(bf)


def deep_gradient(counts, pos, got, early, weight, out, mine):
    w, n = place(pos)
    bx, by = 2 * ((w + 1) // 2) - 2, 2 * ((n + 1) // 2) - 2
    keep = quadrant_keep(128, bx, by, *counts)
    taps = neighbours([got[q, 0:128] for q in range(4)], keep)
    (pooled,) = zsum(dot(weight[...], taps), 64, 32)
    up = exact_up(pooled * 0.125, block_up())
    for s in range(4):
        for x in range(2):
            grad = slope(early[s, 64 * x : 64 * x + 64].astype(f32))
            above = got[s, 128 + 64 * x : 192 + 64 * x].astype(f32)
            value = ((above + up[:, 128 * s : 128 * s + 128]) * grad).astype(bf)
            mine[2 * s + x] = value
    ra, rb = w & 1, n & 1
    for t in range(4):
        for k in range(2):
            a = jnp.where(ra == t // 2, k, 1 - ra)
            b = jnp.where(rb == t % 2, k, 1 - rb)
            for x in range(2):
                at = (2 * k + x) * 64
                out[t, at : at + 64] = mine[(2 * a + b) * 2 + x]


def finish(counts, pos, got, mine, gj, pre, second_b, strips, out, dom, gf, matrix):
    square_matrix(strips, matrix)
    w, n = place(pos)
    ra, rb = w & 1, n & 1

    def put(x, y, tiles):
        inside = flag(w + x - 1, counts[0]) * flag(n + y - 1, counts[1])
        for i, tile in enumerate(tiles):
            dom[2 * x + i, y] = (tile.astype(f32) * inside).astype(bf)

    far_x, far_y = 2 * (1 - ra), 2 * (1 - rb)
    part = lambda q, k: [got[q, (2 * k + i) * 64 : (2 * k + i) * 64 + 64] for i in range(2)]
    for a in range(2):
        for b in range(2):
            put(a + ra, b + rb, [mine[(2 * a + b) * 2 + i] for i in range(2)])
    for k in range(2):
        put(far_x, k + rb, part(2 * (1 - ra) + rb, k))
        put(k + ra, far_y, part(2 * ra + 1 - rb, k))
    put(far_x, far_y, part(2 * (1 - ra) + 1 - rb, 0))
    own = [[dom[row, p] for p in range(3)] for row in range(6)]
    mixed = [[cross(line[o], line[o + 1]) for o in range(2)] for line in own]
    stack = []
    for r in range(4):
        for o in range(2):
            taps = []
            for dx in range(3):
                taps += [own[r + dx][o], mixed[r + dx][o], own[r + dx][o + 1]]
            stack.append(rows_of(taps))
    grads = zsum(dot(second_b[...], cols_of(stack)), 32, 64)
    up = exact_up(rows_of(grads) * 0.125, pair_up())
    fx, fy = edges(pos, counts)
    for x in range(6):
        for y in range(6):
            r, m = (x + 1) // 2, (y + 1) // 2
            at = (2 * r + m // 2) * 32
            value = up[at : at + 32, 128 * (m % 2) : 128 * (m % 2) + 128]
            value = (value + gj[x, y].astype(f32)) * slope(pre[x, y])
            for edge in (fx[x], fy[y]):
                value = value if edge is None else value * edge
            gf[x, y] = value.astype(bf)

    for i in range(2):
        rows = {(dx, y): value for dx, y, value in squares(matrix, gf, 2 * i, 4)}
        for dx in range(2):
            line = jnp.stack([rows[dx, y] for y in range(4)])
            out[:, 2 * i + dx] = jnp.swapaxes(line, 0, 1).astype(bf)


def call(body, counts, outs, scratch, *args):
    smem = pl.BlockSpec(memory_space=pltpu.SMEM)
    vmem = pl.BlockSpec(memory_space=pltpu.VMEM)
    return pl.pallas_call(
        functools.partial(body, counts),
        out_shape=[jax.ShapeDtypeStruct(s, d) for s, d in outs],
        in_specs=[smem] + [vmem] * (len(args) - 1),
        out_specs=[vmem] * len(outs),
        scratch_shapes=[pltpu.VMEM(s, d) for s, d in scratch],
        compiler_params=pltpu.CompilerParams(vmem_limit_bytes=48 * 1024 * 1024),
        cost_estimate=pl.CostEstimate(flops=400000000, bytes_accessed=2000000, transcendentals=0),
    )(*args)


def send(cells, axis, step):
    count = lax.axis_size(axis)
    pairs = [(i, i + step) for i in range(count) if 0 <= i + step < count]
    return lax.ppermute(cells, axis, pairs)


def swap(cells, axis, shift):
    count = lax.axis_size(axis)
    lower = range(shift, count - 1, 2)
    return lax.ppermute(
        cells, axis, [(i, i + 1) for i in lower] + [(i + 1, i) for i in lower]
    )


def shards(
    volume, cotangent, conv_first, conv_second, conv_bottom, lift_weight, conv_decode, conv_final
):
    counts = (lax.axis_size("wide"), lax.axis_size("narrow"))
    pos = jnp.stack([lax.axis_index("wide"), lax.axis_index("narrow")]).astype(jnp.int32)

    def gathered(content, shift):
        groups = [
            [
                ((i + a) % counts[0]) * counts[1] + (j + b) % counts[1]
                for a in range(2)
                for b in range(2)
            ]
            for i in range(shift, counts[0] + shift, 2)
            for j in range(shift, counts[1] + shift, 2)
        ]
        return lax.all_to_all(
            content, ("wide", "narrow"), 0, 0, axis_index_groups=groups
        )

    vol = volume.transpose(1, 2, 0, 3)
    cot = cotangent.transpose(1, 2, 0, 3)
    low = send(jnp.concatenate([vol[:, 1:], cot[:, 2:]], axis=1), "narrow", 1)
    high = send(jnp.concatenate([vol[:, :3], cot[:, :2]], axis=1), "narrow", -1)
    vol = jnp.concatenate([low[:, :3], vol, high[:, :3]], axis=1)
    cot = jnp.concatenate([low[:, 3:], cot, high[:, 3:]], axis=1)
    odd = pos[0] & 1

    def edge(cells, width, side):
        return lax.dynamic_slice_in_dim(cells, side * (4 - width), width, axis=0)

    vol_far = swap(edge(vol, 3, odd), "wide", 1)
    flat = lambda cells: cells.reshape(-1, 32, 128)
    near = [flat(edge(vol, 3, 1 - odd)), flat(edge(cot, 2, 1 - odd))]
    near = swap(jnp.concatenate(near, axis=0), "wide", 0)
    cot_far = swap(edge(cot, 2, odd), "wide", 1)

    matrix = ((384, 512), bf)
    full, cells = (6, 6, 32, 128), (4, 4, 32, 128)
    hid, pre, content, p2 = call(
        encode, counts,
        [(full, bf), (full, f32), ((128, 128), bf), ((4, 64, 128), bf)],
        [((10, 10, 32, 128), bf), ((8, 8, 32, 128), bf), ((8, 6, 32, 128), f32), matrix],
        pos, vol, near, vol_far, forward_strips(conv_first), forward_matrix(conv_second),
    )
    four = gathered(p2, 0)
    gj, total = call(
        adjoint, counts, [(full, bf), ((64, 128), bf)], [((8, 8, 32, 128), bf), matrix],
        pos, cot, near, cot_far, backward_strips(conv_final),
    )
    seg = lax.broadcasted_iota(jnp.int32, (64, 128), 1) // 32
    packed = four[0]
    for q in range(1, 4):
        packed = jnp.where(seg == q, four[q], packed)
    content = jnp.concatenate([content, total, packed], axis=0)
    early = gathered(jnp.broadcast_to(content, (4, 256, 128)), 1)
    (content,) = call(
        bottom, counts, [((736, 128), bf)], [],
        pos, early, forward_matrix(conv_bottom), lift_weight,
    )
    side = swap(content, "narrow", 0)
    chip = swap(content, "wide", 0)
    both = swap(side, "wide", 0)
    content, hidden = call(
        decode, counts, [((4, 256, 128), bf), ((256, 128), bf)],
        [
            ((8, 4, 64, 128), bf), ((8, 3, 64, 128), bf), ((6, 4, 32, 128), bf),
            ((6, 3, 32, 128), f32), ((6, 3, 32, 128), bf), ((4, 2, 64, 128), bf),
            ((4, 736, 128), bf),
        ],
        pos, content, chip, side, both, forward_matrix(conv_decode), backward_matrix(conv_decode), lift_weight.T,
    )
    got = gathered(content, 1)
    (features,) = call(
        output, counts, [(cells, bf)], [(full, bf), matrix],
        pos, hidden, hid, forward_strips(conv_final),
    )
    content, mine = call(
        deep_gradient, counts, [((4, 256, 128), bf), ((8, 64, 128), bf)], [],
        pos, got, early, backward_matrix(conv_bottom),
    )
    got = gathered(content, 0)
    (grad,) = call(
        finish, counts, [((32, 4, 4, 128), bf)], [((6, 3, 64, 128), bf), (full, bf), matrix],
        pos, got, mine, gj, pre, backward_matrix(conv_second), backward_strips(conv_first),
    )
    return features.transpose(2, 0, 1, 3), grad


def solution(mesh):
    field = P(None, "wide", "narrow", None)

    return jax.shard_map(
        shards,
        mesh=mesh,
        in_specs=(field, field) + (P(),) * 6,
        out_specs=(field, field),
        check_vma=False,
    )
```
